256 devices in a mesh: seq: 16 (over z, core), head: 16 (over y, x).
Axes of the slice: x: 4, y: 4, z: 8, core: 2. Of those that a mesh axis runs over, the one named last changes fastest.
Arguments:
- queries: bfloat16 [49152, 32, 128], P('seq', 'head'), may hold values from -6 to 6
- keys: bfloat16 [49152, 32, 128], P('seq', 'head'), may hold values from -6 to 6
- values: bfloat16 [49152, 32, 128], P('seq', 'head'), may hold values from -60 to 60
- cotangent: bfloat16 [49152, 32, 128], P('seq', 'head'), may hold values from -6 to 6
- doc_lengths: int32 [6], replicated, may hold values from 1 to 36864, 49152 in all
Outputs:
- output: bfloat16 [49152, 32, 128], P('seq', 'head')
- grad_queries: bfloat16 [49152, 32, 128], P('seq', 'head')
- grad_keys: bfloat16 [49152, 32, 128], P('seq', 'head')
- grad_values: bfloat16 [49152, 32, 128], P('seq', 'head')
The draws below stay inside these ranges and needn't reach their ends.
All inputs are finite; a program needn't handle non-finite values.
Results may differ from the reference program's by a relative error of at most 0.0058.
Values sent between devices are 32-bit elements; how exact they have to be, the bound alone decides.
A program may use at most 128 MiB of HBM per device.

```python
import math
import jax
import jax.numpy as jnp
import numpy as np
from jax import lax

DH = 128
GROUP = 256
NDOCS = 6
TOK_DEV = 3072
TOKENS = 49152
HEADS = 32


def draw_values(key, part):
    noise_key, head_key, row_key = jax.random.split(key, 3)
    head_place = jnp.arange(HEADS, dtype=jnp.float32)
    head_scale = 10.0 ** ((head_place + jax.random.uniform(head_key, (HEADS,), dtype=jnp.float32)) / HEADS - 0.5)
    unit_noise = jnp.clip(jax.random.normal(noise_key, (TOKENS, HEADS, DH), dtype=jnp.float32), -6.0, 6.0)
    row_scale = jnp.exp(jax.random.uniform(row_key, (TOKENS,), dtype=jnp.float32, minval=math.log(0.3), maxval=math.log(3.0)))
    return (unit_noise * row_scale[:, None, None] * head_scale[None, :, None]).astype(jnp.bfloat16)


def block_scale(key, extent, pieces, low, largest):
    def one(position, shards_of):
        heights = jax.random.uniform(jax.random.fold_in(jax.random.fold_in(key, 6), position), (shards_of,), jnp.float32, low / len(pieces), largest / len(pieces))
        return jnp.repeat(jnp.exp(heights), extent[position] // shards_of).reshape((-1,) + (1,) * (len(extent) - position - 1))

    gain = one(*pieces[0])
    for cut in pieces[1:]:
        gain = gain * one(*cut)
    return gain


def length_profile(count, total, bound, skew):
    portions = [(1 << 20) // math.isqrt(rank ** skew) + 1 for rank in range(2, count + 1)]
    surplus, counts = total - bound - (count - 1), [1] * (count - 1)
    while surplus > 0:
        free = [i for i in range(count - 1) if counts[i] < bound]
        whole, remaining = sum([portions[i] for i in free]), surplus
        for i in free:
            extra = min(bound - counts[i], max(1, remaining * portions[i] // whole), surplus)
            counts[i] = counts[i] + extra
            surplus = surplus - extra
    return np.array([bound] + counts)


def ragged_sizes(own_key, number_of, total, bound, slope):
    if number_of == 2:
        one = jax.random.randint(own_key, (), max(1, total - bound), min(bound, total - 1) + 1)
        return jnp.stack([one, total - one])
    lengths = jnp.asarray(length_profile(number_of, total, bound, slope), jnp.int32)
    couples = (number_of - 1) // 2
    donor, sink = lengths[1:1 + 2 * couples:2], lengths[2:2 + 2 * couples:2]
    slack = jnp.minimum(donor - 1, bound - sink)
    shifted = jax.random.randint(jax.random.fold_in(own_key, 1), (couples,), 0, 1 << 20) % (slack + 1)
    lengths = lengths.at[1:1 + 2 * couples:2].set(donor - shifted).at[2:2 + 2 * couples:2].set(sink + shifted)
    return lengths[jax.random.permutation(jax.random.fold_in(own_key, 2), number_of)]


def normal_values(own_key, shape, spread, most, cuts=(), held_as=jnp.bfloat16):
    values = spread * jax.random.normal(own_key, shape, jnp.float32)
    if cuts:
        values = values * block_scale(own_key, shape, cuts, -0.22, 0.18)
    return jnp.clip(values, -most, most).astype(held_as)


def setup_inputs(seed: int = 0) -> dict:
    seeds = jax.random.split(jax.random.key(seed), 6)
    return {
        "queries": normal_values(seeds[0], (TOKENS, HEADS, DH), 1.0, 6.0, ((0, 16), (1, 16))),
        "keys": normal_values(seeds[1], (TOKENS, HEADS, DH), 1.0, 6.0, ((0, 16), (1, 16))),
        "values": draw_values(jax.random.fold_in(seeds[5], 71), 0),
        "cotangent": normal_values(seeds[3], (TOKENS, HEADS, DH), 1.0, 6.0, ((0, 16), (1, 16))),
        "doc_lengths": ragged_sizes(seeds[4], NDOCS, TOKENS, 3 * TOKENS // 4, 1).astype(jnp.int32),
    }


EPSILON = 1e-06

def segment_of(places, doc_ends):
    return lax.optimization_barrier(jnp.sum((doc_ends[None, :] <= places[:, None]).astype(jnp.int32), axis=1))

def rounded(array):
    return lax.optimization_barrier(array.astype(jnp.bfloat16)).astype(jnp.float32)

def reference(queries, keys, values, cotangent, doc_lengths):
    doc_ends = jnp.cumsum(doc_lengths).astype(jnp.int32)
    n_groups = TOKENS // GROUP
    per_shard = TOK_DEV // GROUP
    width_all = float(HEADS * DH)

    def blocks(array):
        return array.reshape(n_groups, GROUP, HEADS, DH)
    query_blocks = blocks(queries)
    key_blocks = blocks(keys)
    value_blocks = blocks(values)
    grad_blocks = blocks(cotangent)
    positions = jnp.arange(TOKENS, dtype=jnp.int32)
    segment = segment_of(positions, doc_ends).reshape(n_groups, GROUP)
    group_ids = jnp.arange(n_groups, dtype=jnp.int32)
    group_first = group_ids * GROUP
    before_group = segment_of(group_first - 1, doc_ends)
    after_group = segment_of(group_first + GROUP, doc_ends)
    shard_first = group_ids // per_shard * TOK_DEV
    before_shard = segment_of(shard_first - 1, doc_ends)
    after_shard = segment_of(shard_first + TOK_DEV, doc_ends)
    opens = group_ids % per_shard == 0
    closes = group_ids % per_shard == per_shard - 1
    causal = jnp.arange(GROUP)[:, None] >= jnp.arange(GROUP)[None, :]
    zero_state = jnp.zeros((HEADS, DH, DH), jnp.float32)

    def group_probs(query_f, key_f, segment_group):
        within = causal & (segment_group[:, None] == segment_group[None, :])
        scores = jnp.einsum('thd,shd->hts', query_f, key_f)
        return (within, rounded(jnp.where(within[None], scores, 0.0)))

    def forward_step(running, inputs):
        state_in, state_local, last_before = running
        query_group, key_group, value_group, grad_group, segment_group, before_c, before_s, opening = inputs
        joined = jnp.where(before_s == last_before, state_in, 0.0) + state_local
        state_in = jnp.where(opening, joined, state_in)
        state_local = jnp.where(opening, 0.0, state_local)
        query_f = query_group.astype(jnp.float32)
        key_f = key_group.astype(jnp.float32)
        value_f = value_group.astype(jnp.float32)
        within, probs = group_probs(query_f, key_f, segment_group)
        local_bf = rounded(state_local)
        remote_bf = rounded(state_in)
        gate_local = (segment_group == before_c).astype(jnp.float32)[:, None, None]
        gate_remote = (segment_group == before_s).astype(jnp.float32)[:, None, None]
        mixed = jnp.einsum('hts,shd->thd', probs, value_f)
        mixed = mixed + gate_local * jnp.einsum('thi,hij->thj', query_f, local_bf)
        mixed = mixed + gate_remote * jnp.einsum('thi,hij->thj', query_f, remote_bf)
        squares = lax.optimization_barrier(jnp.sum(mixed * mixed, axis=(1, 2)))
        root = jnp.sqrt(squares / width_all + EPSILON)
        normed = mixed / root[:, None, None]
        grad_f = grad_group.astype(jnp.float32)
        centre = lax.optimization_barrier(jnp.sum(grad_f * normed, axis=(1, 2))) / width_all
        grad_mixed = ((grad_f - normed * centre[:, None, None]) / root[:, None, None]).astype(jnp.bfloat16)
        grad_mf = lax.optimization_barrier(grad_mixed).astype(jnp.float32)
        grad_probs = rounded(jnp.where(within[None], jnp.einsum('thd,shd->hts', grad_mf, value_f), 0.0))
        grad_query = jnp.einsum('hts,shd->thd', grad_probs, key_f)
        grad_query = grad_query + gate_local * jnp.einsum('thj,hij->thi', grad_mf, local_bf)
        grad_query = grad_query + gate_remote * jnp.einsum('thj,hij->thi', grad_mf, remote_bf)
        ending = segment_group[-1]
        tail = (segment_group == ending).astype(jnp.float32)[:, None, None]
        added = jnp.einsum('thi,thj->hij', key_f * tail, value_f)
        state_local = jnp.where(ending == before_c, state_local, 0.0) + added
        return ((state_in, state_local, before_s), (normed.astype(jnp.bfloat16), grad_query.astype(jnp.bfloat16), grad_mixed))
    start_before = segment_of(jnp.array([-1], dtype=jnp.int32), doc_ends)[0]
    inputs = (query_blocks, key_blocks, value_blocks, grad_blocks, segment, before_group, before_shard, opens)
    _, (output, grad_queries, grad_mixed_all) = lax.scan(forward_step, (zero_state, zero_state, start_before), inputs)

    def backward_step(running, inputs):
        state_in, state_local, last_after = running
        query_group, key_group, value_group, grad_group, segment_group, after_c, after_s, closing = inputs
        joined = jnp.where(after_s == last_after, state_in, 0.0) + state_local
        state_in = jnp.where(closing, joined, state_in)
        state_local = jnp.where(closing, 0.0, state_local)
        query_f = query_group.astype(jnp.float32)
        key_f = key_group.astype(jnp.float32)
        value_f = value_group.astype(jnp.float32)
        grad_mf = grad_group.astype(jnp.float32)
        within, probs = group_probs(query_f, key_f, segment_group)
        grad_probs = rounded(jnp.where(within[None], jnp.einsum('thd,shd->hts', grad_mf, value_f), 0.0))
        local_bf = rounded(state_local)
        remote_bf = rounded(state_in)
        gate_local = (segment_group == after_c).astype(jnp.float32)[:, None, None]
        gate_remote = (segment_group == after_s).astype(jnp.float32)[:, None, None]
        grad_key = jnp.einsum('hts,thd->shd', grad_probs, query_f)
        grad_key = grad_key + gate_local * jnp.einsum('shj,hij->shi', value_f, local_bf)
        grad_key = grad_key + gate_remote * jnp.einsum('shj,hij->shi', value_f, remote_bf)
        grad_value = jnp.einsum('hts,thd->shd', probs, grad_mf)
        grad_value = grad_value + gate_local * jnp.einsum('shi,hij->shj', key_f, local_bf)
        grad_value = grad_value + gate_remote * jnp.einsum('shi,hij->shj', key_f, remote_bf)
        leading = segment_group[0]
        head_part = (segment_group == leading).astype(jnp.float32)[:, None, None]
        added = jnp.einsum('thi,thj->hij', query_f * head_part, grad_mf)
        state_local = jnp.where(leading == after_c, state_local, 0.0) + added
        return ((state_in, state_local, after_s), (grad_key.astype(jnp.bfloat16), grad_value.astype(jnp.bfloat16)))
    start_after = segment_of(jnp.array([TOKENS], dtype=jnp.int32), doc_ends)[0]
    inputs = (query_blocks, key_blocks, value_blocks, grad_mixed_all, segment, after_group, after_shard, closes)
    _, (grad_keys, grad_values) = lax.scan(backward_step, (zero_state, zero_state, start_after), inputs, reverse=True)
    shape = (TOKENS, HEADS, DH)
    return (output.reshape(shape), grad_queries.reshape(shape), grad_keys.reshape(shape), grad_values.reshape(shape))
```

```python
import functools

import jax
import jax.numpy as jnp
from jax import lax
from jax.experimental import pallas as pl
from jax.experimental.pallas import tpu as pltpu
from jax.sharding import PartitionSpec as P

GROUP = 256
EPSILON = 1e-06
MESH = pl.DeviceIdType.MESH
F32 = jnp.float32
BF16 = jnp.bfloat16


def dot(a, b, ca=1, cb=0):
    return lax.dot_general(a, b, (((ca,), (cb,)), ((), ())), preferred_element_type=F32)


def kernel(
    sizes,
    doc_ref,
    q_hbm,
    k_hbm,
    v_hbm,
    g_hbm,
    out_hbm,
    dq_hbm,
    dk_hbm,
    dv_hbm,
    raw,
    tmp,
    heads,
    mask_ref,
    gates,
    p_ref,
    o_ref,
    dob_ref,
    dkl_ref,
    dvl_ref,
    stage_f,
    stage_b,
    s_loc,
    s_bf,
    r_loc,
    s_run,
    s_got,
    s_pre,
    s_in,
    r_run,
    r_got,
    r_pre,
    r_in,
    part,
    x_got,
    x_sum,
    y_got,
    tot,
    in_sem,
    out_sem,
    s_send,
    s_recv,
    t_send,
    t_recv,
    r_send,
    r_recv,
    u_send,
    u_recv,
    x_send,
    x_recv,
    y_send,
    y_recv,
):
    n_seq, n_x, n_y, n_groups, n_heads = sizes
    tokens = n_groups * GROUP
    rows2 = GROUP * n_heads
    width_all = float(n_x * n_y * n_heads * 128)
    me = lax.axis_index("seq")
    head = lax.axis_index("head")
    mx = lax.rem(head, n_x)
    my = head // n_x
    slab = n_heads * 128 // n_seq

    def head_of(x, y):
        return y * n_x + x

    barrier = pltpu.get_barrier_semaphore()
    for d in range(1, n_seq):
        pl.semaphore_signal(barrier, inc=1, device_id={"seq": lax.rem(me + d, n_seq)}, device_id_type=MESH)
    for d in range(1, n_x):
        pl.semaphore_signal(
            barrier, inc=1, device_id={"head": head_of(lax.rem(mx + d, n_x), my)}, device_id_type=MESH
        )
    for d in range(1, n_y):
        pl.semaphore_signal(
            barrier, inc=1, device_id={"head": head_of(mx, lax.rem(my + d, n_y))}, device_id_type=MESH
        )

    sources = (k_hbm, v_hbm, q_hbm, g_hbm)
    KK, VV, QQ, GG = range(4)

    def load(a, g):
        return pltpu.make_async_copy(sources[a].at[g], raw.at[a, g], in_sem.at[a, g])

    @pl.loop(0, n_groups)
    def _(g):
        load(KK, g).start()
        load(VV, g).start()

    @pl.loop(0, n_groups)
    def _(g):
        load(QQ, g).start()
        load(GG, g).start()

    ends = []
    total = 0
    for j in range(doc_ref.shape[0]):
        total = total + doc_ref[j]
        ends.append(total)

    def seg_of(p):
        s = (ends[0] <= p).astype(jnp.int32)
        for e in ends[1:]:
            s = s + (e <= p).astype(jnp.int32)
        return s

    def flag(cond):
        return jnp.where(cond, 1.0, 0.0).astype(F32)

    shard_first = me * tokens
    bs = seg_of(shard_first - 1)
    after_s = seg_of(shard_first + tokens)

    def edges(g):
        first = shard_first + g * GROUP
        return seg_of(first - 1), seg_of(first), seg_of(first + GROUP - 1), seg_of(first + GROUP)

    GB, GT, GH, GA = range(4)

    @pl.loop(0, n_groups)
    def _(g):
        first = shard_first + g * GROUP
        bc, c0, c1, ac = edges(g)
        row = lax.broadcasted_iota(jnp.int32, (GROUP, 128), 0)
        seg_r = seg_of(row + first)
        col = lax.broadcasted_iota(jnp.int32, (8, GROUP), 1)
        seg_c = seg_of(col + first)[0:1]
        for half in range(2):
            lane = lax.broadcasted_iota(jnp.int32, (GROUP, 128), 1) + half * 128
            same = seg_r == jnp.broadcast_to(seg_c[:, half * 128 : half * 128 + 128], (GROUP, 128))
            mask_ref[g, :, half * 128 : half * 128 + 128] = jnp.where(
                jnp.logical_and(same, row >= lane), 1.0, 0.0
            ).astype(F32)
        for i, ref_seg in ((GB, bc), (GT, c1), (GH, c0), (GA, ac)):
            gates[i, g] = jnp.where(seg_r == ref_seg, 1.0, 0.0).astype(BF16)

    def split(a, g):
        tmp[a] = raw[a, g].astype(F32)
        for h in range(n_heads):
            heads[a, h, g] = tmp[a, pl.ds(h, GROUP, stride=n_heads), :].astype(BF16)

    s_run[...] = jnp.zeros_like(s_run)

    @pl.loop(0, n_groups)
    def _(g):
        bc, c0, c1, ac = edges(g)
        load(KK, g).wait()
        load(VV, g).wait()
        split(KK, g)
        split(VV, g)
        keep = flag(c1 == bc)
        for h in range(n_heads):
            added = dot(heads[KK, h, g] * gates[GT, g], heads[VV, h, g], 0, 0)
            old = s_run[h]
            s_loc[h, g] = old
            s_run[h] = keep * old + added

    pl.semaphore_wait(barrier, n_seq - 1 + n_x - 1 + n_y - 1)

    def hand(src, dst, send, recv, d):
        peer = lax.rem(me + d, n_seq)
        return pltpu.make_async_remote_copy(
            src_ref=src(peer),
            dst_ref=dst,
            send_sem=send.at[d],
            recv_sem=recv.at[me],
            device_id={"seq": peer},
            device_id_type=MESH,
        )

    def arrived(dst, send, recv, d):
        peer = lax.rem(me + d, n_seq)
        return pltpu.make_async_remote_copy(
            src_ref=dst(peer),
            dst_ref=dst(peer),
            send_sem=send.at[d],
            recv_sem=recv.at[peer],
            device_id={"seq": peer},
            device_id_type=MESH,
        )

    def rows(ref, i):
        return ref.at[pl.ds(pl.multiple_of(i * slab, slab), slab)]

    def scatter(run2d, got, send, recv):
        for d in range(1, n_seq):
            hand(lambda p: rows(run2d, p), got.at[me], send, recv, d).start()

    def scatter_done(run2d, got, send, recv):
        for d in range(1, n_seq):
            hand(lambda p: rows(run2d, p), got.at[me], send, recv, d).wait_send()
            arrived(lambda p: got.at[p], send, recv, d).wait_recv()

    def give(pre, into, send, recv):
        for d in range(1, n_seq):
            hand(lambda p: pre.at[p], rows(into, me), send, recv, d).start()

    def give_done(pre, into, send, recv):
        for d in range(1, n_seq):
            hand(lambda p: pre.at[p], rows(into, me), send, recv, d).wait_send()
            arrived(lambda p: rows(into, p), send, recv, d).wait_recv()

    def combine(run2d, got, pre, into, backward):
        got[me] = run2d[pl.ds(pl.multiple_of(me * slab, slab), slab), :]
        carry = jnp.zeros((slab, 128), F32)
        order = range(n_seq - 1, -1, -1) if backward else range(n_seq)
        for i in order:
            pre[i] = carry
            first = i * tokens
            if backward:
                keep = flag(seg_of(first) == seg_of(first + tokens))
            else:
                keep = flag(seg_of(first + tokens - 1) == seg_of(first - 1))
            carry = keep * carry + got[i]
        into[pl.ds(pl.multiple_of(me * slab, slab), slab), :] = pre[me]

    def flat(ref):
        return ref.reshape(n_heads * 128, 128)

    scatter(flat(s_run), s_got, s_send, s_recv)

    def intra(g):
        load(QQ, g).wait()
        split(QQ, g)
        for h in range(n_heads):
            scores = dot(heads[QQ, h, g], heads[KK, h, g], 1, 1)
            probs = (scores * mask_ref[g]).astype(BF16)
            p_ref[h, g] = probs
            o_ref[h, g] = dot(probs, heads[VV, h, g])

    half = n_groups // 2

    @pl.loop(0, half)
    def _(g):
        intra(g)

    scatter_done(flat(s_run), s_got, s_send, s_recv)
    combine(flat(s_run), s_got, s_pre, s_in, False)
    give(s_pre, s_in, t_send, t_recv)

    @pl.loop(half, n_groups)
    def _(g):
        intra(g)

    @pl.loop(0, n_groups)
    def _(g):
        load(GG, g).wait()
        split(GG, g)

    give_done(s_pre, s_in, t_send, t_recv)

    ones = jnp.ones((16, n_heads * 128), BF16)

    @pl.loop(0, n_groups)
    def _(g):
        bc, c0, c1, ac = edges(g)
        w = flag(bc == bs)
        squares, inner = [], []
        for h in range(n_heads):
            state = (s_loc[h, g] + w * s_in[h * 128 : h * 128 + 128, :]).astype(BF16)
            s_bf[h, g] = state
            o = o_ref[h, g] + dot(heads[QQ, h, g] * gates[GB, g], state)
            o_ref[h, g] = o
            squares.append((o * o).astype(BF16))
            inner.append((heads[GG, h, g].astype(F32) * o).astype(BF16))
        part[pl.ds(g, 1), :] = dot(ones, jnp.concatenate(squares, axis=1), 1, 1)[0:1]
        part[pl.ds(n_groups + g, 1), :] = dot(ones, jnp.concatenate(inner, axis=1), 1, 1)[0:1]

    def ring(axis_x, src, got, send, recv, d, wait):
        n, mine = (n_x, mx) if axis_x else (n_y, my)
        other = lax.rem(mine + d, n)
        peer = head_of(other, my) if axis_x else head_of(mx, other)
        slot = other if wait else mine
        return pltpu.make_async_remote_copy(
            src_ref=src,
            dst_ref=got.at[slot],
            send_sem=send.at[d],
            recv_sem=recv.at[slot],
            device_id={"head": peer},
            device_id_type=MESH,
        )

    def reduce_over(axis_x, src, got, send, recv, into):
        n, mine = (n_x, mx) if axis_x else (n_y, my)
        for d in range(1, n):
            ring(axis_x, src, got, send, recv, d, False).start()
        got[mine] = src[...]
        for d in range(1, n):
            ring(axis_x, src, got, send, recv, d, False).wait_send()
            ring(axis_x, src, got, send, recv, d, True).wait_recv()
        value = got[0]
        for i in range(1, n):
            value = value + got[i]
        into[...] = value

    reduce_over(True, part, x_got, x_send, x_recv, x_sum)
    reduce_over(False, x_sum, y_got, y_send, y_recv, tot)

    r_run[...] = jnp.zeros_like(r_run)
    sub = lax.broadcasted_iota(jnp.int32, (16, 256), 0)
    lane = lax.broadcasted_iota(jnp.int32, (16, 256), 1)
    spread = jnp.where(
        jnp.logical_or(
            jnp.logical_and(sub < 2, lane < 128),
            jnp.logical_and(jnp.logical_and(sub >= 2, sub < 4), lane >= 128),
        ),
        1.0,
        0.0,
    ).astype(BF16)
    sub_t = lax.broadcasted_iota(jnp.int32, (16, GROUP), 0)

    @pl.loop(0, n_groups)
    def _(step):
        g = n_groups - 1 - step
        bc, c0, c1, ac = edges(g)
        sq = tot[pl.ds(g, 1), :]
        gd = tot[pl.ds(n_groups + g, 1), :]
        a = 1.0 / jnp.sqrt(sq / width_all + EPSILON)
        c = a * a * (a * gd / width_all)
        a_hi = a.astype(BF16).astype(F32)
        c_hi = c.astype(BF16).astype(F32)
        wide = lambda x: jnp.broadcast_to(x, (16, GROUP))
        terms = jnp.where(
            sub_t == 0,
            wide(a_hi),
            jnp.where(
                sub_t == 1,
                wide(a - a_hi),
                jnp.where(sub_t == 2, wide(c_hi), jnp.where(sub_t == 3, wide(c - c_hi), 0.0)),
            ),
        ).astype(BF16)
        both = dot(terms, spread, 0, 0)
        aa, cc = both[:, :128], both[:, 128:]
        keep = flag(c0 == ac)
        for h in range(n_heads):
            o = o_ref[h, g]
            stage_f[0, g, pl.ds(h, GROUP, stride=n_heads), :] = o * aa
            dob = (heads[GG, h, g].astype(F32) * aa - o * cc).astype(BF16)
            dob_ref[h, g] = dob
            added = dot(heads[QQ, h, g] * gates[GH, g], dob, 0, 0)
            old = r_run[h]
            r_loc[h, g] = old
            r_run[h] = keep * old + added

    scatter(flat(r_run), r_got, r_send, r_recv)

    targets = (out_hbm, dq_hbm, dk_hbm, dv_hbm)

    def store(i, g):
        return pltpu.make_async_copy(stage_b.at[i, g], targets[i].at[g], out_sem.at[i, g])

    def emit(i, g):
        stage_b[i, g] = stage_f[i, g].astype(BF16)
        store(i, g).start()

    def inner_back(g):
        emit(0, g)
        for h in range(n_heads):
            dob = dob_ref[h, g]
            dp = (dot(dob, heads[VV, h, g], 1, 1) * mask_ref[g]).astype(BF16)
            dq = dot(dp, heads[KK, h, g]) + dot(dob * gates[GB, g], s_bf[h, g], 1, 1)
            stage_f[1, g, pl.ds(h, GROUP, stride=n_heads), :] = dq
            dkl_ref[h, g] = dot(dp, heads[QQ, h, g], 0, 0)
            dvl_ref[h, g] = dot(p_ref[h, g], dob, 0, 0)
        emit(1, g)

    @pl.loop(0, half)
    def _(g):
        inner_back(g)

    scatter_done(flat(r_run), r_got, r_send, r_recv)
    combine(flat(r_run), r_got, r_pre, r_in, True)
    give(r_pre, r_in, u_send, u_recv)

    @pl.loop(half, n_groups)
    def _(g):
        inner_back(g)

    give_done(r_pre, r_in, u_send, u_recv)

    @pl.loop(0, n_groups)
    def _(g):
        bc, c0, c1, ac = edges(g)
        w = flag(ac == after_s)
        for h in range(n_heads):
            state = (r_loc[h, g] + w * r_in[h * 128 : h * 128 + 128, :]).astype(BF16)
            stage_f[2, g, pl.ds(h, GROUP, stride=n_heads), :] = dkl_ref[h, g] + dot(
                heads[VV, h, g] * gates[GA, g], state, 1, 1
            )
            stage_f[3, g, pl.ds(h, GROUP, stride=n_heads), :] = dvl_ref[h, g] + dot(
                heads[KK, h, g] * gates[GA, g], state
            )
        emit(2, g)
        emit(3, g)

    @pl.loop(0, n_groups)
    def _(g):
        for i in range(4):
            store(i, g).wait()


def per_device(sizes, queries, keys, values, cotangent, doc_lengths):
    tokens_here, n_heads, width = queries.shape
    n_seq, n_x, n_y = sizes
    n_groups = tokens_here // GROUP
    rows2 = GROUP * n_heads
    slab = n_heads * 128 // n_seq
    view = lambda x: x.reshape(n_groups, rows2, width)
    out = jax.ShapeDtypeStruct((n_groups, rows2, width), BF16)
    dma = pltpu.SemaphoreType.DMA
    vm = pltpu.VMEM
    per_head = (n_heads, n_groups, GROUP, width)
    states = (n_heads, n_groups, width, width)
    exchange = [
        vm((n_heads, width, width), F32),
        vm((n_seq, slab, width), F32),
        vm((n_seq, slab, width), F32),
        vm((n_heads * width, width), F32),
    ]
    sums = (2 * n_groups, GROUP)
    results = pl.pallas_call(
        functools.partial(kernel, (n_seq, n_x, n_y, n_groups, n_heads)),
        out_shape=(out,) * 4,
        in_specs=[pl.BlockSpec(memory_space=pltpu.SMEM)] + [pl.BlockSpec(memory_space=pl.ANY)] * 4,
        out_specs=(pl.BlockSpec(memory_space=pl.ANY),) * 4,
        scratch_shapes=[
            vm((4, n_groups, rows2, width), BF16),
            vm((4, rows2, width), F32),
            vm((4,) + per_head, BF16),
            vm((n_groups, GROUP, GROUP), F32),
            vm((4, n_groups, GROUP, width), BF16),
            vm((n_heads, n_groups, GROUP, GROUP), BF16),
            vm(per_head, F32),
            vm(per_head, BF16),
            vm(per_head, F32),
            vm(per_head, F32),
            vm((4, n_groups, rows2, width), F32),
            vm((4, n_groups, rows2, width), BF16),
            vm(states, F32),
            vm(states, BF16),
            vm(states, F32),
        ]
        + exchange
        + exchange
        + [
            vm(sums, F32),
            vm((n_x,) + sums, F32),
            vm(sums, F32),
            vm((n_y,) + sums, F32),
            vm(sums, F32),
            dma((4, n_groups)),
            dma((4, n_groups)),
        ]
        + [dma((n_seq,))] * 8
        + [dma((n_x,))] * 2
        + [dma((n_y,))] * 2,
        compiler_params=pltpu.CompilerParams(
            collective_id=0, has_side_effects=True, vmem_limit_bytes=64000 * 1024
        ),
    )(doc_lengths, view(queries), view(keys), view(values), view(cotangent))
    return tuple(r.reshape(tokens_here, n_heads, width) for r in results)


def solution(mesh):
    n_x = 4
    spec = P("seq", "head", None)
    return jax.shard_map(
        functools.partial(per_device, (mesh.shape["seq"], n_x, mesh.shape["head"] // n_x)),
        mesh=mesh,
        in_specs=(spec,) * 4 + (P(),),
        out_specs=(spec,) * 4,
        check_vma=False,
    )
```

```python
import functools

import jax
import jax.numpy as jnp
from jax import lax
from jax.experimental import pallas as pl
from jax.experimental.pallas import tpu as pltpu
from jax.sharding import PartitionSpec as P

GROUP = 256
EPSILON = 1e-06
CHUNK = 4
MESH = pl.DeviceIdType.MESH
F32 = jnp.float32
BF16 = jnp.bfloat16
KK, VV = range(2)
QQ, GG = range(2)


def dot(a, b, ca=1, cb=0):
    return lax.dot_general(a, b, (((ca,), (cb,)), ((), ())), preferred_element_type=F32)


def flag(cond):
    return jnp.where(cond, 1.0, 0.0).astype(F32)


def doc_ends(doc_ref):
    ends, total = [], 0
    for j in range(doc_ref.shape[0]):
        total = total + doc_ref[j]
        ends.append(total)
    return ends


def seg_of(ends, p):
    s = (ends[0] <= p).astype(jnp.int32)
    for e in ends[1:]:
        s = s + (e <= p).astype(jnp.int32)
    return s


def last_end(ends, p):
    s = jnp.where(ends[0] <= p, ends[0], 0)
    for e in ends[1:]:
        s = jnp.where(e <= p, e, s)
    return s


def next_end(ends, p):
    s = ends[-1]
    for e in ends[-2::-1]:
        s = jnp.where(e > p, e, s)
    return s


def row_gate(lower, limit):
    row = lax.broadcasted_iota(jnp.int32, (GROUP, 128), 0)
    return jnp.where(row >= limit if lower else row < limit, 1.0, 0.0).astype(BF16)


def far_first(n, per_chip):
    chips = n // per_chip

    def hops(d):
        c = d // per_chip
        return min(c, chips - c)

    return sorted(range(1, n), key=lambda d: -hops(d))


def main_kernel(
    sizes,
    doc_ref,
    q_hbm,
    k_hbm,
    v_hbm,
    g_hbm,
    out_v,
    dq_v,
    dkl_ref,
    dvl_ref,
    kv,
    r_loc,
    r_in,
    raw,
    tmp,
    qg,
    mask_ref,
    p_ref,
    o_ref,
    dob_ref,
    stage,
    s_loc,
    s_bf,
    keep_ref,
    s_run,
    s_got,
    s_pre,
    s_in,
    r_run,
    r_got,
    r_pre,
    part,
    t_got,
    tot,
    in_sem,
    s_send,
    s_recv,
    t_send,
    t_recv,
    r_send,
    r_recv,
    u_send,
    u_recv,
    a_send,
    a_recv,
):
    n_seq, n_x, n_y, n_groups, n_heads = sizes
    tokens = n_groups * GROUP
    n_head = n_x * n_y
    width_all = float(n_head * n_heads * 128)
    n_chunks = n_groups // CHUNK
    me = lax.axis_index("seq")
    head = lax.axis_index("head")
    mx = lax.rem(head, n_x)
    my = head // n_x
    slab = 128 // n_seq
    seq_order = far_first(n_seq, 2)
    head_order = sorted(
        range(1, n_head),
        key=lambda d: -(min(d % n_x, n_x - d % n_x) + min(d // n_x, n_y - d // n_x)),
    )

    def seq_peer(d):
        return lax.rem(me + d, n_seq)

    def head_peer(d, sign):
        x = lax.rem(mx + n_x + sign * (d % n_x), n_x)
        y = lax.rem(my + n_y + sign * (d // n_x), n_y)
        return y * n_x + x

    barrier = pltpu.get_barrier_semaphore()
    for d in seq_order:
        pl.semaphore_signal(barrier, inc=1, device_id={"seq": seq_peer(d)}, device_id_type=MESH)
    for d in head_order:
        pl.semaphore_signal(barrier, inc=1, device_id={"head": head_peer(d, 1)}, device_id_type=MESH)

    sources = (k_hbm, v_hbm, q_hbm, g_hbm)

    def load(a, g):
        return pltpu.make_async_copy(sources[a].at[g], raw.at[a, g], in_sem.at[a, g])

    @pl.loop(0, n_groups)
    def _(g):
        load(0, g).start()
        load(1, g).start()

    @pl.loop(0, n_groups)
    def _(g):
        load(2, g).start()
        load(3, g).start()

    ends = doc_ends(doc_ref)
    shard_first = me * tokens
    bs = seg_of(ends, shard_first - 1)

    def edges(g):
        first = shard_first + g * GROUP
        return (
            seg_of(ends, first - 1),
            seg_of(ends, first),
            seg_of(ends, first + GROUP - 1),
            seg_of(ends, first + GROUP),
        )

    def before_gate(g):
        first = shard_first + g * GROUP
        return row_gate(False, next_end(ends, first - 1) - first)

    def tail_gate(g):
        first = shard_first + g * GROUP
        return row_gate(True, last_end(ends, first + GROUP - 1) - first)

    def lead_gate(g):
        first = shard_first + g * GROUP
        return row_gate(False, next_end(ends, first) - first)

    for i in range(n_seq):
        first = i * tokens
        keep_ref[0, i] = flag(seg_of(ends, first + tokens - 1) == seg_of(ends, first - 1))
        keep_ref[1, i] = flag(seg_of(ends, first) == seg_of(ends, first + tokens))

    def split(a, g, into, i):
        tmp[a] = raw[a, g].astype(F32)
        for h in range(n_heads):
            into[i, h, g] = tmp[a, pl.ds(h, GROUP, stride=n_heads), :].astype(BF16)

    def key_state(g, h):
        bc, c0, c1, ac = edges(g)
        added = dot(kv[KK, h, g] * tail_gate(g), kv[VV, h, g], 0, 0)
        old = s_run[h]
        s_loc[h, g] = old
        s_run[h] = flag(c1 == bc) * old + added

    def hand(src, dst, send, recv, d):
        return pltpu.make_async_remote_copy(
            src_ref=src,
            dst_ref=dst,
            send_sem=send.at[d],
            recv_sem=recv.at[me],
            device_id={"seq": seq_peer(d)},
            device_id_type=MESH,
        )

    def taken(dst, send, recv, d):
        return pltpu.make_async_remote_copy(
            src_ref=dst,
            dst_ref=dst,
            send_sem=send.at[d],
            recv_sem=recv.at[seq_peer(d)],
            device_id={"seq": seq_peer(d)},
            device_id_type=MESH,
        )

    def rows(ref, h, i):
        return ref.at[h, pl.ds(pl.multiple_of(i * slab, slab), slab)]

    def scatter(h, run, got, send, recv):
        for d in seq_order:
            hand(rows(run, h, seq_peer(d)), got.at[h, me], send.at[h], recv.at[h], d).start()

    def combine(h, run, got, pre, into, send, recv, backward):
        mine = pl.ds(pl.multiple_of(me * slab, slab), slab)
        got[h, me] = run[h, mine, :]
        for d in reversed(seq_order):
            taken(got.at[h, seq_peer(d)], send.at[h], recv.at[h], d).wait_recv()
        carry = jnp.zeros((slab, 128), F32)
        for i in range(n_seq - 1, -1, -1) if backward else range(n_seq):
            pre[h, i] = carry
            carry = keep_ref[1 if backward else 0, i] * carry + got[h, i]
        into[h, mine, :] = pre[h, me]

    def give(h, pre, into, send, recv):
        for d in seq_order:
            hand(pre.at[h, seq_peer(d)], rows(into, h, me), send.at[h], recv.at[h], d).start()

    def give_done(h, into, send, recv):
        for d in reversed(seq_order):
            taken(rows(into, h, seq_peer(d)), send.at[h], recv.at[h], d).wait_recv()

    def sends_done(h, run, got, send, recv, pre, into, send2, recv2):
        for d in seq_order:
            hand(rows(run, h, seq_peer(d)), got.at[h, me], send.at[h], recv.at[h], d).wait_send()
            hand(pre.at[h, seq_peer(d)], rows(into, h, me), send2.at[h], recv2.at[h], d).wait_send()

    s_run[...] = jnp.zeros_like(s_run)
    part[...] = jnp.zeros_like(part)

    @pl.loop(0, n_groups)
    def _(g):
        load(0, g).wait()
        load(1, g).wait()
        split(0, g, kv, KK)
        split(1, g, kv, VV)
        key_state(g, 0)

    pl.semaphore_wait(barrier, n_seq - 1 + n_head - 1)
    scatter(0, s_run, s_got, s_send, s_recv)

    for h in range(1, n_heads):

        @pl.loop(0, n_groups)
        def _(g):
            key_state(g, h)

        scatter(h, s_run, s_got, s_send, s_recv)

    @pl.loop(0, n_groups)
    def _(g):
        first = shard_first + g * GROUP
        row = lax.broadcasted_iota(jnp.int32, (GROUP, 128), 0)
        start = last_end(ends, row + first) - first
        for half in range(2):
            lane = lax.broadcasted_iota(jnp.int32, (GROUP, 128), 1) + half * 128
            mask_ref[g, :, half * 128 : half * 128 + 128] = jnp.where(
                jnp.logical_and(lane >= start, row >= lane), 1.0, 0.0
            ).astype(F32)

    def intra(g):
        load(2, g).wait()
        split(2, g, qg, QQ)
        for h in range(n_heads):
            scores = dot(qg[QQ, h, g], kv[KK, h, g], 1, 1)
            probs = (scores * mask_ref[g]).astype(BF16)
            p_ref[h, g] = probs
            o_ref[h, g] = dot(probs, kv[VV, h, g])

    cut1, cut2 = (2 * n_groups) // 3, (5 * n_groups) // 6

    @pl.loop(0, cut1)
    def _(g):
        intra(g)

    combine(0, s_run, s_got, s_pre, s_in, s_send, s_recv, False)
    give(0, s_pre, s_in, t_send, t_recv)

    @pl.loop(cut1, cut2)
    def _(g):
        intra(g)

    for h in range(1, n_heads):
        combine(h, s_run, s_got, s_pre, s_in, s_send, s_recv, False)
        give(h, s_pre, s_in, t_send, t_recv)

    @pl.loop(cut2, n_groups)
    def _(g):
        intra(g)

    @pl.loop(0, n_groups)
    def _(g):
        load(3, g).wait()
        split(3, g, qg, GG)

    ones = jnp.ones((16, 128), BF16)

    def outer(g, h):
        bc, c0, c1, ac = edges(g)
        w = flag(bc == bs)
        state = (s_loc[h, g] + w * s_in[h]).astype(BF16)
        s_bf[h, g] = state
        o = o_ref[h, g] + dot(qg[QQ, h, g] * before_gate(g), state)
        o_ref[h, g] = o
        c, r = g // CHUNK, lax.rem(g, CHUNK)
        squares = dot(ones, (o * o).astype(BF16), 1, 1)[0:1]
        inner = dot(ones, (qg[GG, h, g].astype(F32) * o).astype(BF16), 1, 1)[0:1]
        part[c, pl.ds(r, 1), :] += squares
        part[c, pl.ds(CHUNK + r, 1), :] += inner

    for h in range(n_heads - 1):
        give_done(h, s_in, t_send, t_recv)

        @pl.loop(0, n_groups)
        def _(g):
            outer(g, h)

    give_done(n_heads - 1, s_in, t_send, t_recv)

    def part_copy(c, d, wait):
        slot = head_peer(d, 1) if wait else head
        return pltpu.make_async_remote_copy(
            src_ref=part.at[c],
            dst_ref=t_got.at[c, slot],
            send_sem=a_send.at[c, d],
            recv_sem=a_recv.at[c, slot],
            device_id={"head": head_peer(d, 1)},
            device_id_type=MESH,
        )

    for c in range(n_chunks - 1, -1, -1):

        @pl.loop(0, CHUNK)
        def _(r):
            outer(c * CHUNK + r, n_heads - 1)

        for d in head_order:
            part_copy(c, d, False).start()
        t_got[c, head] = part[c]

    r_run[...] = jnp.zeros_like(r_run)
    sub = lax.broadcasted_iota(jnp.int32, (16, 256), 0)
    lane = lax.broadcasted_iota(jnp.int32, (16, 256), 1)
    spread = jnp.where(
        jnp.logical_or(
            jnp.logical_and(sub < 2, lane < 128),
            jnp.logical_and(jnp.logical_and(sub >= 2, sub < 4), lane >= 128),
        ),
        1.0,
        0.0,
    ).astype(BF16)
    sub_t = lax.broadcasted_iota(jnp.int32, (16, GROUP), 0)

    def scales(g):
        c, r = g // CHUNK, lax.rem(g, CHUNK)
        sq = tot[c, pl.ds(r, 1), :]
        gd = tot[c, pl.ds(CHUNK + r, 1), :]
        a = 1.0 / jnp.sqrt(sq / width_all + EPSILON)
        b = a * a * (a * gd / width_all)
        a_hi = a.astype(BF16).astype(F32)
        b_hi = b.astype(BF16).astype(F32)
        wide = lambda x: jnp.broadcast_to(x, (16, GROUP))
        terms = jnp.where(
            sub_t == 0,
            wide(a_hi),
            jnp.where(
                sub_t == 1,
                wide(a - a_hi),
                jnp.where(sub_t == 2, wide(b_hi), jnp.where(sub_t == 3, wide(b - b_hi), 0.0)),
            ),
        ).astype(BF16)
        both = dot(terms, spread, 0, 0)
        return both[:, :128], both[:, 128:]

    def back_state(g, aa, bb, h):
        bc, c0, c1, ac = edges(g)
        dob = (qg[GG, h, g].astype(F32) * aa - o_ref[h, g] * bb).astype(BF16)
        dob_ref[h, g] = dob
        added = dot(qg[QQ, h, g] * lead_gate(g), dob, 0, 0)
        old = r_run[h]
        r_loc[h, g] = old
        r_run[h] = flag(c0 == ac) * old + added

    def gather_part(c):
        for d in reversed(head_order):
            part_copy(c, d, True).wait_recv()
        value = t_got[c, 0]
        for i in range(1, n_head):
            value = value + t_got[c, i]
        tot[c] = value

    for c in range(n_chunks - 1, 0, -1):
        gather_part(c)

        @pl.loop(0, CHUNK)
        def _(step):
            g = c * CHUNK + CHUNK - 1 - step
            aa, bb = scales(g)
            for h in range(n_heads):
                back_state(g, aa, bb, h)

    gather_part(0)
    for h in range(n_heads):

        @pl.loop(0, CHUNK)
        def _(step):
            g = CHUNK - 1 - step
            aa, bb = scales(g)
            back_state(g, aa, bb, h)

        scatter(h, r_run, r_got, r_send, r_recv)

    def inner_back(g):
        aa, _ = scales(g)
        before = before_gate(g)
        for h in range(n_heads):
            even = pl.ds(h, GROUP, stride=n_heads)
            stage[0, even, :] = o_ref[h, g] * aa
            dob = dob_ref[h, g]
            dp = (dot(dob, kv[VV, h, g], 1, 1) * mask_ref[g]).astype(BF16)
            dq = dot(dp, kv[KK, h, g]) + dot(dob * before, s_bf[h, g], 1, 1)
            stage[1, even, :] = dq
            dkl_ref[h, g] = dot(dp, qg[QQ, h, g], 0, 0)
            dvl_ref[h, g] = dot(p_ref[h, g], dob, 0, 0)
        out_v[g] = stage[0].astype(BF16)
        dq_v[g] = stage[1].astype(BF16)

    cut1, cut2 = (2 * n_groups) // 3, (5 * n_groups) // 6

    @pl.loop(0, cut1)
    def _(g):
        inner_back(g)

    combine(0, r_run, r_got, r_pre, r_in, r_send, r_recv, True)
    give(0, r_pre, r_in, u_send, u_recv)

    @pl.loop(cut1, cut2)
    def _(g):
        inner_back(g)

    for h in range(1, n_heads):
        combine(h, r_run, r_got, r_pre, r_in, r_send, r_recv, True)
        give(h, r_pre, r_in, u_send, u_recv)

    @pl.loop(cut2, n_groups)
    def _(g):
        inner_back(g)

    for h in range(n_heads):
        sends_done(h, s_run, s_got, s_send, s_recv, s_pre, s_in, t_send, t_recv)
    for c in range(n_chunks):
        for d in head_order:
            part_copy(c, d, False).wait_send()
    for h in range(n_heads):
        give_done(h, r_in, u_send, u_recv)
        sends_done(h, r_run, r_got, r_send, r_recv, r_pre, r_in, u_send, u_recv)


def last_kernel(
    sizes,
    doc_ref,
    out_v,
    dq_v,
    dkl_ref,
    dvl_ref,
    kv,
    r_loc,
    r_in,
    out_hbm,
    dq_hbm,
    dk_hbm,
    dv_hbm,
    stage,
    done,
    sem,
    whole,
):
    n_seq, n_x, n_y, n_groups, n_heads = sizes
    tokens = n_groups * GROUP
    shard_first = lax.axis_index("seq") * tokens
    copies = [
        pltpu.make_async_copy(out_v, out_hbm, whole.at[0]),
        pltpu.make_async_copy(dq_v, dq_hbm, whole.at[1]),
    ]
    for c in copies:
        c.start()
    ends = doc_ends(doc_ref)
    after_s = seg_of(ends, shard_first + tokens)
    targets = (dk_hbm, dv_hbm)

    def store(i, g):
        return pltpu.make_async_copy(done.at[i, g], targets[i].at[g], sem.at[i, g])

    @pl.loop(0, n_groups)
    def _(g):
        first = shard_first + g * GROUP
        w = flag(seg_of(ends, first + GROUP) == after_s)
        after = row_gate(True, last_end(ends, first + GROUP) - first)
        for h in range(n_heads):
            even = pl.ds(h, GROUP, stride=n_heads)
            state = (r_loc[h, g] + w * r_in[h]).astype(BF16)
            stage[0, even, :] = dkl_ref[h, g] + dot(kv[VV, h, g] * after, state, 1, 1)
            stage[1, even, :] = dvl_ref[h, g] + dot(kv[KK, h, g] * after, state)
        for i in range(2):
            done[i, g] = stage[i].astype(BF16)
            store(i, g).start()

    @pl.loop(0, n_groups)
    def _(g):
        for i in range(2):
            store(i, g).wait()

    for c in copies:
        c.wait()


def per_device(sizes, queries, keys, values, cotangent, doc_lengths):
    tokens_here, n_heads, width = queries.shape
    n_seq, n_x, n_y = sizes
    n_groups = tokens_here // GROUP
    n_chunks = n_groups // CHUNK
    rows2 = GROUP * n_heads
    slab = width // n_seq
    sizes = (n_seq, n_x, n_y, n_groups, n_heads)
    view = lambda x: x.reshape(n_groups, rows2, width)
    dma = pltpu.SemaphoreType.DMA
    vm = pltpu.VMEM
    anywhere = pl.BlockSpec(memory_space=pl.ANY)
    on_chip = pl.BlockSpec(memory_space=pltpu.VMEM)
    scalars = pl.BlockSpec(memory_space=pltpu.SMEM)
    per_head = (n_heads, n_groups, GROUP, width)
    states = (n_heads, n_groups, width, width)
    one_state = (n_heads, width, width)
    slices = (n_heads, n_seq, slab, width)
    sums = (n_chunks, 2 * CHUNK, GROUP)
    packed = (n_groups, rows2, width)
    mids = pl.pallas_call(
        functools.partial(main_kernel, sizes),
        out_shape=(
            vm(packed, BF16),
            vm(packed, BF16),
            vm(per_head, F32),
            vm(per_head, F32),
            vm((2,) + per_head, BF16),
            vm(states, F32),
            vm(one_state, F32),
        ),
        in_specs=[scalars] + [anywhere] * 4,
        out_specs=(on_chip,) * 7,
        scratch_shapes=[
            vm((4,) + packed, BF16),
            vm((4, rows2, width), F32),
            vm((2,) + per_head, BF16),
            vm((n_groups, GROUP, GROUP), F32),
            vm((n_heads, n_groups, GROUP, GROUP), BF16),
            vm(per_head, F32),
            vm(per_head, BF16),
            vm((2, rows2, width), F32),
            vm(states, F32),
            vm(states, BF16),
            pltpu.SMEM((2, n_seq), F32),
            vm(one_state, F32),
            vm(slices, F32),
            vm(slices, F32),
            vm(one_state, F32),
            vm(one_state, F32),
            vm(slices, F32),
            vm(slices, F32),
            vm(sums, F32),
            vm((n_chunks, n_x * n_y, 2 * CHUNK, GROUP), F32),
            vm(sums, F32),
            dma((4, n_groups)),
        ]
        + [dma((n_heads, n_seq))] * 8
        + [dma((n_chunks, n_x * n_y))] * 2,
        compiler_params=pltpu.CompilerParams(
            collective_id=0, has_side_effects=True, vmem_limit_bytes=44 << 20
        ),
        name="exchange_and_attend",
    )(doc_lengths, view(queries), view(keys), view(values), view(cotangent))
    mids = [pltpu.with_memory_space_constraint(m, pltpu.VMEM) for m in mids]
    results = pl.pallas_call(
        functools.partial(last_kernel, sizes),
        out_shape=(jax.ShapeDtypeStruct(packed, BF16),) * 4,
        in_specs=[scalars] + [on_chip] * 7,
        out_specs=(anywhere,) * 4,
        scratch_shapes=[
            vm((2, rows2, width), F32),
            vm((2,) + packed, BF16),
            dma((2, n_groups)),
            dma((2,)),
        ],
        compiler_params=pltpu.CompilerParams(vmem_limit_bytes=16 << 20),
        name="finish",
    )(doc_lengths, *mids)
    return tuple(r.reshape(tokens_here, n_heads, width) for r in results)


def solution(mesh):
    n_x = 4
    spec = P("seq", "head", None)
    return jax.shard_map(
        functools.partial(per_device, (mesh.shape["seq"], n_x, mesh.shape["head"] // n_x)),
        mesh=mesh,
        in_specs=(spec,) * 4 + (P(),),
        out_specs=(spec,) * 4,
        check_vma=False,
    )
```

```python
import functools

import jax
import jax.numpy as jnp
from jax import lax
from jax.experimental import pallas as pl
from jax.experimental.pallas import tpu as pltpu
from jax.sharding import PartitionSpec as P

GROUP = 256
EPSILON = 1e-06
CHUNK = 4
MESH = pl.DeviceIdType.MESH
F32 = jnp.float32
BF16 = jnp.bfloat16
KK, VV = range(2)
QQ, GG = range(2)


def dot(a, b, ca=1, cb=0):
    return lax.dot_general(a, b, (((ca,), (cb,)), ((), ())), preferred_element_type=F32)


def flag(cond):
    return jnp.where(cond, 1.0, 0.0).astype(F32)


def doc_ends(doc_ref):
    ends, total = [], 0
    for j in range(doc_ref.shape[0]):
        total = total + doc_ref[j]
        ends.append(total)
    return ends


def seg_of(ends, p):
    s = (ends[0] <= p).astype(jnp.int32)
    for e in ends[1:]:
        s = s + (e <= p).astype(jnp.int32)
    return s


def last_end(ends, p):
    s = jnp.where(ends[0] <= p, ends[0], 0)
    for e in ends[1:]:
        s = jnp.where(e <= p, e, s)
    return s


def next_end(ends, p):
    s = ends[-1]
    for e in ends[-2::-1]:
        s = jnp.where(e > p, e, s)
    return s


def lane_gate(lower, limit):
    lane = lax.broadcasted_iota(jnp.int32, (16, GROUP), 1)
    one = jnp.where(lane >= limit if lower else lane < limit, 1.0, 0.0).astype(BF16)
    return jnp.concatenate([one] * 8, axis=0)


def far_first(n, per_chip):
    chips = n // per_chip

    def hops(d):
        c = d // per_chip
        return min(c, chips - c)

    return sorted(range(1, n), key=lambda d: -hops(d))


def main_kernel(
    sizes,
    doc_ref,
    q_hbm,
    k_hbm,
    v_hbm,
    g_hbm,
    out_v,
    dq_v,
    dk_t,
    dv_t,
    k_t,
    v_t,
    r_loc,
    r_in,
    raw,
    tmp,
    k_n,
    v_n,
    q_t,
    g_t,
    mask_ref,
    p_t,
    dp_t,
    o_t,
    dob_t,
    stage,
    s_loc,
    s_bf,
    keep_ref,
    s_got,
    s_pre,
    s_in,
    r_got,
    r_pre,
    part,
    t_got,
    scale_a,
    scale_b,
    in_sem,
    s_send,
    s_recv,
    t_send,
    t_recv,
    r_send,
    r_recv,
    u_send,
    u_recv,
    a_send,
    a_recv,
):
    n_seq, n_x, n_y, n_groups, n_heads = sizes
    tokens = n_groups * GROUP
    n_head = n_x * n_y
    width_all = float(n_head * n_heads * 128)
    n_chunks = n_groups // CHUNK
    me = lax.axis_index("seq")
    head = lax.axis_index("head")
    mx = lax.rem(head, n_x)
    my = head // n_x
    slab = 128 // n_seq
    seq_order = far_first(n_seq, 2)
    head_order = sorted(
        range(1, n_head),
        key=lambda d: -(min(d % n_x, n_x - d % n_x) + min(d // n_x, n_y - d // n_x)),
    )

    def seq_peer(d):
        return lax.rem(me + d, n_seq)

    def head_peer(d, sign):
        x = lax.rem(mx + n_x + sign * (d % n_x), n_x)
        y = lax.rem(my + n_y + sign * (d // n_x), n_y)
        return y * n_x + x

    sources = (k_hbm, v_hbm, q_hbm, g_hbm)

    def load(a, g):
        return pltpu.make_async_copy(sources[a].at[g], raw.at[a, g], in_sem.at[a, g])

    @pl.loop(0, n_groups)
    def _(g):
        load(0, g).start()
        load(1, g).start()

    @pl.loop(0, n_groups)
    def _(g):
        load(2, g).start()
        load(3, g).start()

    barrier = pltpu.get_barrier_semaphore()
    for d in seq_order:
        pl.semaphore_signal(barrier, inc=1, device_id={"seq": seq_peer(d)}, device_id_type=MESH)
    for d in head_order:
        pl.semaphore_signal(barrier, inc=1, device_id={"head": head_peer(d, 1)}, device_id_type=MESH)

    ends = doc_ends(doc_ref)
    shard_first = me * tokens
    bs = seg_of(ends, shard_first - 1)

    def edges(g):
        first = shard_first + g * GROUP
        return (
            seg_of(ends, first - 1),
            seg_of(ends, first),
            seg_of(ends, first + GROUP - 1),
            seg_of(ends, first + GROUP),
        )

    def before_gate(g):
        first = shard_first + g * GROUP
        return lane_gate(False, next_end(ends, first - 1) - first)

    def tail_gate(g):
        first = shard_first + g * GROUP
        return lane_gate(True, last_end(ends, first + GROUP - 1) - first)

    def lead_gate(g):
        first = shard_first + g * GROUP
        return lane_gate(False, next_end(ends, first) - first)

    both_heads = range(n_heads)

    def spread(a, g, slot):
        tmp[slot] = raw[a, g].astype(F32)
        return [tmp[slot, pl.ds(h, GROUP, stride=n_heads), :].astype(BF16) for h in both_heads]

    def join(slot, parts):
        for h in both_heads:
            stage[slot, pl.ds(h, GROUP, stride=n_heads), :] = parts[h].astype(BF16).T.astype(F32)
        return stage[slot].astype(BF16)

    def key_states(groups, h):
        added = [dot(v_t[h, g] * tail_gate(g), k_n[h, g]) for g in groups]
        for g, new in zip(groups, added):
            bc, c0, c1, ac = edges(g)
            s_loc[h, g + 1] = flag(c1 == bc) * s_loc[h, g] + new

    def hand(src, dst, send, recv, d):
        return pltpu.make_async_remote_copy(
            src_ref=src,
            dst_ref=dst,
            send_sem=send.at[d],
            recv_sem=recv.at[me],
            device_id={"seq": seq_peer(d)},
            device_id_type=MESH,
        )

    def taken(dst, send, recv, d):
        return pltpu.make_async_remote_copy(
            src_ref=dst,
            dst_ref=dst,
            send_sem=send.at[d],
            recv_sem=recv.at[seq_peer(d)],
            device_id={"seq": seq_peer(d)},
            device_id_type=MESH,
        )

    def rows(ref, h, i):
        return ref.at[h, pl.ds(pl.multiple_of(i * slab, slab), slab)]

    class Run:
        def __init__(self, ref, slot):
            self.ref, self.slot = ref, slot

        @property
        def at(self):
            return self

        def __getitem__(self, index):
            h, rest = index
            return self.ref.at[h, self.slot, rest]

    s_run, r_run = Run(s_loc, n_groups), Run(r_loc, 0)

    def scatter(h, run, got, send, recv):
        for d in seq_order:
            hand(rows(run, h, seq_peer(d)), got.at[h, me], send.at[h], recv.at[h], d).start()

    def combine(h, run, got, pre, into, send, recv, backward):
        mine = pl.ds(pl.multiple_of(me * slab, slab), slab)
        got[h, me] = run.ref[h, run.slot, mine, :]
        for d in reversed(seq_order):
            taken(got.at[h, seq_peer(d)], send.at[h], recv.at[h], d).wait_recv()
        carry = jnp.zeros((slab, 128), F32)
        for i in range(n_seq - 1, -1, -1) if backward else range(n_seq):
            pre[h, i] = carry
            carry = keep_ref[1 if backward else 0, i] * carry + got[h, i]
        into[h, mine, :] = pre[h, me]

    def give(h, pre, into, send, recv):
        for d in seq_order:
            hand(pre.at[h, seq_peer(d)], rows(into, h, me), send.at[h], recv.at[h], d).start()

    def give_done(h, into, send, recv):
        for d in reversed(seq_order):
            taken(rows(into, h, seq_peer(d)), send.at[h], recv.at[h], d).wait_recv()

    def sends_done(h, run, got, send, recv, pre, into, send2, recv2):
        for d in seq_order:
            hand(rows(run, h, seq_peer(d)), got.at[h, me], send.at[h], recv.at[h], d).wait_send()
            hand(pre.at[h, seq_peer(d)], rows(into, h, me), send2.at[h], recv2.at[h], d).wait_send()

    pair = 2
    for h in both_heads:
        s_loc[h, 0] = jnp.zeros((128, 128), F32)

    @pl.loop(0, n_groups // pair)
    def _(i):
        groups = [i * pair + u for u in range(pair)]
        for g in groups:
            load(0, g).wait()
            load(1, g).wait()
        for u, g in enumerate(groups):
            for h, x in enumerate(spread(0, g, 2 * u)):
                k_n[h, g] = x
            for h, x in enumerate(spread(1, g, 2 * u + 1)):
                v_n[h, g] = x
                v_t[h, g] = x.T
        key_states(groups, 0)

    pl.semaphore_wait(barrier, n_seq - 1 + n_head - 1)
    scatter(0, s_run, s_got, s_send, s_recv)

    for h in range(1, n_heads):

        @pl.loop(0, n_groups // CHUNK)
        def _(i):
            key_states([i * CHUNK + u for u in range(CHUNK)], h)

        scatter(h, s_run, s_got, s_send, s_recv)

    for i in range(n_seq):
        first = i * tokens
        keep_ref[0, i] = flag(seg_of(ends, first + tokens - 1) == seg_of(ends, first - 1))
        keep_ref[1, i] = flag(seg_of(ends, first) == seg_of(ends, first + tokens))

    def build_mask(g):
        first = shard_first + g * GROUP
        lane8 = lax.broadcasted_iota(jnp.int32, (8, GROUP), 1)
        start = jnp.broadcast_to((last_end(ends, lane8 + first) - first)[0:1], (GROUP, GROUP))
        key = lax.broadcasted_iota(jnp.int32, (GROUP, GROUP), 0)
        query = lax.broadcasted_iota(jnp.int32, (GROUP, GROUP), 1)
        mask_ref[g] = jnp.where(jnp.logical_and(key >= start, key <= query), 1.0, 0.0).astype(F32)

    def intra(i):
        groups = [i * pair + u for u in range(pair)]
        for u, g in enumerate(groups):
            load(2, g).wait()
            build_mask(g)
            for h, x in enumerate(spread(2, g, u)):
                q_t[h, g] = x.T
                k_t[h, g] = k_n[h, g].T
        for g in groups:
            for h in both_heads:
                p_t[h, g] = (dot(k_n[h, g], q_t[h, g]) * mask_ref[g]).astype(BF16)
        for g in groups:
            for h in both_heads:
                o_t[h, g] = dot(v_t[h, g], p_t[h, g])

    n_pairs = n_groups // pair
    cut1, cut2 = (2 * n_pairs) // 3, (5 * n_pairs) // 6

    @pl.loop(0, cut1)
    def _(i):
        intra(i)

    combine(0, s_run, s_got, s_pre, s_in, s_send, s_recv, False)
    give(0, s_pre, s_in, t_send, t_recv)

    @pl.loop(cut1, cut2)
    def _(i):
        intra(i)

    for h in range(1, n_heads):
        combine(h, s_run, s_got, s_pre, s_in, s_send, s_recv, False)
        give(h, s_pre, s_in, t_send, t_recv)

    @pl.loop(cut2, n_pairs)
    def _(i):
        intra(i)

    @pl.loop(0, n_pairs)
    def _(i):
        groups = [i * pair + u for u in range(pair)]
        for u, g in enumerate(groups):
            load(3, g).wait()
            for h, x in enumerate(spread(3, g, u)):
                g_t[h, g] = x.T

    def outer(groups, h):
        for g in groups:
            bc, c0, c1, ac = edges(g)
            s_bf[h, g] = (s_loc[h, g] + flag(bc == bs) * s_in[h]).astype(BF16)
        more = [dot(s_bf[h, g], q_t[h, g] * before_gate(g)) for g in groups]
        for g, x in zip(groups, more):
            o = o_t[h, g] + x
            o_t[h, g] = o
            c, r = g // CHUNK, lax.rem(g, CHUNK)
            squares = jnp.sum(o * o, axis=0, keepdims=True)
            inner = jnp.sum(g_t[h, g].astype(F32) * o, axis=0, keepdims=True)
            one, two = pl.ds(r, 1), pl.ds(CHUNK + r, 1)
            if h == 0:
                part[c, one, :] = squares
                part[c, two, :] = inner
            else:
                part[c, one, :] += squares
                part[c, two, :] += inner

    for h in range(n_heads - 1):
        give_done(h, s_in, t_send, t_recv)

        @pl.loop(0, n_pairs)
        def _(i):
            outer([i * pair + u for u in range(pair)], h)

    give_done(n_heads - 1, s_in, t_send, t_recv)

    def part_copy(c, d, wait):
        slot = head_peer(d, 1) if wait else head
        return pltpu.make_async_remote_copy(
            src_ref=part.at[c],
            dst_ref=t_got.at[c, slot],
            send_sem=a_send.at[c, d],
            recv_sem=a_recv.at[c, slot],
            device_id={"head": head_peer(d, 1)},
            device_id_type=MESH,
        )

    for c in range(n_chunks - 1, -1, -1):

        @pl.loop(0, CHUNK // pair)
        def _(i):
            outer([c * CHUNK + i * pair + u for u in range(pair)], n_heads - 1)

        for d in head_order:
            part_copy(c, d, False).start()
        t_got[c, head] = part[c]

    for h in both_heads:
        r_loc[h, n_groups] = jnp.zeros((128, 128), F32)

    def wide(ref, g):
        c, r = g // CHUNK, lax.rem(g, CHUNK)
        return jnp.broadcast_to(ref[c, pl.ds(r, 1), :], (128, GROUP))

    def back_states(groups, heads):
        for g in groups:
            for h in heads:
                dob_t[h, g] = (g_t[h, g].astype(F32) * wide(scale_a, g) - o_t[h, g] * wide(scale_b, g)).astype(BF16)
        added = [[dot(q_t[h, g] * lead_gate(g), dob_t[h, g], 1, 1) for h in heads] for g in groups]
        for g, row in zip(groups, added):
            bc, c0, c1, ac = edges(g)
            for h, new in zip(heads, row):
                r_loc[h, g] = flag(c0 == ac) * r_loc[h, g + 1] + new

    def gather_part(c):
        for d in reversed(head_order):
            part_copy(c, d, True).wait_recv()
        value = t_got[c, 0]
        for i in range(1, n_head):
            value = value + t_got[c, i]
        a = 1.0 / jnp.sqrt(value[:CHUNK] / width_all + EPSILON)
        scale_a[c, 0:CHUNK] = a
        scale_b[c, 0:CHUNK] = a * a * (a * value[CHUNK:] / width_all)

    for c in range(n_chunks - 1, 0, -1):
        gather_part(c)

        @pl.loop(0, CHUNK // pair)
        def _(i):
            top = c * CHUNK + CHUNK - 1 - i * pair
            back_states([top - u for u in range(pair)], both_heads)

    gather_part(0)
    for h in both_heads:

        @pl.loop(0, CHUNK // pair)
        def _(i):
            top = CHUNK - 1 - i * pair
            back_states([top - u for u in range(pair)], [h])

        scatter(h, r_run, r_got, r_send, r_recv)

    def inner_back(g):
        before = before_gate(g)
        for h in both_heads:
            dp_t[h] = (dot(v_n[h, g], dob_t[h, g]) * mask_ref[g]).astype(BF16)
        for h in both_heads:
            dv_t[h, g] = dot(dob_t[h, g], p_t[h, g], 1, 1)
        out_v[g] = join(0, [o_t[h, g] * wide(scale_a, g) for h in both_heads])
        more = [dot(s_bf[h, g], dob_t[h, g] * before, 0, 0) for h in both_heads]
        dq_v[g] = join(1, [dot(k_t[h, g], dp_t[h]) + more[h] for h in both_heads])
        for h in both_heads:
            dk_t[h, g] = dot(q_t[h, g], dp_t[h], 1, 1)

    cut1, cut2 = (2 * n_groups) // 3, (5 * n_groups) // 6

    @pl.loop(0, cut1)
    def _(g):
        inner_back(g)

    combine(0, r_run, r_got, r_pre, r_in, r_send, r_recv, True)
    give(0, r_pre, r_in, u_send, u_recv)

    @pl.loop(cut1, cut2)
    def _(g):
        inner_back(g)

    for h in range(1, n_heads):
        combine(h, r_run, r_got, r_pre, r_in, r_send, r_recv, True)
        give(h, r_pre, r_in, u_send, u_recv)

    @pl.loop(cut2, n_groups)
    def _(g):
        inner_back(g)

    for h in both_heads:
        sends_done(h, s_run, s_got, s_send, s_recv, s_pre, s_in, t_send, t_recv)
    for c in range(n_chunks):
        for d in head_order:
            part_copy(c, d, False).wait_send()
    for h in both_heads:
        give_done(h, r_in, u_send, u_recv)
        sends_done(h, r_run, r_got, r_send, r_recv, r_pre, r_in, u_send, u_recv)


def last_kernel(
    sizes,
    doc_ref,
    out_v,
    dq_v,
    dk_t,
    dv_t,
    k_t,
    v_t,
    r_loc,
    r_in,
    out_hbm,
    dq_hbm,
    dk_hbm,
    dv_hbm,
    stage,
    done,
    sem,
    whole,
):
    n_seq, n_x, n_y, n_groups, n_heads = sizes
    tokens = n_groups * GROUP
    shard_first = lax.axis_index("seq") * tokens
    copies = [
        pltpu.make_async_copy(out_v, out_hbm, whole.at[0]),
        pltpu.make_async_copy(dq_v, dq_hbm, whole.at[1]),
    ]
    for c in copies:
        c.start()
    ends = doc_ends(doc_ref)
    after_s = seg_of(ends, shard_first + tokens)
    targets = (dk_hbm, dv_hbm)
    pair = 2

    def store(i, g):
        return pltpu.make_async_copy(done.at[i, g], targets[i].at[g], sem.at[i, g])

    @pl.loop(0, n_groups // pair)
    def _(step):
        todo = []
        for u in range(pair):
            g = step * pair + u
            first = shard_first + g * GROUP
            w = flag(seg_of(ends, first + GROUP) == after_s)
            after = lane_gate(True, last_end(ends, first + GROUP) - first)
            for h in range(n_heads):
                state = (r_loc[h, g + 1] + w * r_in[h]).astype(BF16)
                todo.append((0, u, g, h, dk_t, dot(state, v_t[h, g] * after)))
                todo.append((1, u, g, h, dv_t, dot(state, k_t[h, g] * after, 0, 0)))
        for i, u, g, h, base, x in todo:
            block = (base[h, g] + x).astype(BF16).T.astype(F32)
            stage[2 * u + i, pl.ds(h, GROUP, stride=n_heads), :] = block
        for u in range(pair):
            for i in range(2):
                g = step * pair + u
                done[i, g] = stage[2 * u + i].astype(BF16)
                store(i, g).start()

    @pl.loop(0, n_groups)
    def _(g):
        for i in range(2):
            store(i, g).wait()

    for c in copies:
        c.wait()


def per_device(sizes, queries, keys, values, cotangent, doc_lengths):
    tokens_here, n_heads, width = queries.shape
    n_seq, n_x, n_y = sizes
    n_groups = tokens_here // GROUP
    n_chunks = n_groups // CHUNK
    rows2 = GROUP * n_heads
    slab = width // n_seq
    sizes = (n_seq, n_x, n_y, n_groups, n_heads)
    view = lambda x: x.reshape(n_groups, rows2, width)
    dma = pltpu.SemaphoreType.DMA
    vm = pltpu.VMEM
    anywhere = pl.BlockSpec(memory_space=pl.ANY)
    on_chip = pl.BlockSpec(memory_space=pltpu.VMEM)
    scalars = pl.BlockSpec(memory_space=pltpu.SMEM)
    per_head = (n_heads, n_groups, GROUP, width)
    turned = (n_heads, n_groups, width, GROUP)
    states = (n_heads, n_groups + 1, width, width)
    one_state = (n_heads, width, width)
    slices = (n_heads, n_seq, slab, width)
    sums = (n_chunks, 2 * CHUNK, GROUP)
    packed = (n_groups, rows2, width)
    mids = pl.pallas_call(
        functools.partial(main_kernel, sizes),
        out_shape=(
            vm(packed, BF16),
            vm(packed, BF16),
            vm(turned, F32),
            vm(turned, F32),
            vm(turned, BF16),
            vm(turned, BF16),
            vm(states, F32),
            vm(one_state, F32),
        ),
        in_specs=[scalars] + [anywhere] * 4,
        out_specs=(on_chip,) * 8,
        scratch_shapes=[
            vm((4,) + packed, BF16),
            vm((4, rows2, width), F32),
            vm(per_head, BF16),
            vm(per_head, BF16),
            vm(turned, BF16),
            vm(turned, BF16),
            vm((n_groups, GROUP, GROUP), F32),
            vm((n_heads, n_groups, GROUP, GROUP), BF16),
            vm((n_heads, GROUP, GROUP), BF16),
            vm(turned, F32),
            vm(turned, BF16),
            vm((2, rows2, width), F32),
            vm(states, F32),
            vm((n_heads, n_groups, width, width), BF16),
            pltpu.SMEM((2, n_seq), F32),
            vm(slices, F32),
            vm(slices, F32),
            vm(one_state, F32),
            vm(slices, F32),
            vm(slices, F32),
            vm(sums, F32),
            vm((n_chunks, n_x * n_y, 2 * CHUNK, GROUP), F32),
            vm(sums, F32),
            vm(sums, F32),
            dma((4, n_groups)),
        ]
        + [dma((n_heads, n_seq))] * 8
        + [dma((n_chunks, n_x * n_y))] * 2,
        compiler_params=pltpu.CompilerParams(
            collective_id=0, has_side_effects=True, vmem_limit_bytes=44 << 20
        ),
        name="exchange_and_attend",
    )(doc_lengths, view(queries), view(keys), view(values), view(cotangent))
    mids = [pltpu.with_memory_space_constraint(m, pltpu.VMEM) for m in mids]
    results = pl.pallas_call(
        functools.partial(last_kernel, sizes),
        out_shape=(jax.ShapeDtypeStruct(packed, BF16),) * 4,
        in_specs=[scalars] + [on_chip] * 8,
        out_specs=(anywhere,) * 4,
        scratch_shapes=[
            vm((4, rows2, width), F32),
            vm((2,) + packed, BF16),
            dma((2, n_groups)),
            dma((2,)),
        ],
        compiler_params=pltpu.CompilerParams(vmem_limit_bytes=16 << 20),
        name="finish",
    )(doc_lengths, *mids)
    return tuple(r.reshape(tokens_here, n_heads, width) for r in results)


def solution(mesh):
    n_x = 4
    spec = P("seq", "head", None)
    return jax.shard_map(
        functools.partial(per_device, (mesh.shape["seq"], n_x, mesh.shape["head"] // n_x)),
        mesh=mesh,
        in_specs=(spec,) * 4 + (P(),),
        out_specs=(spec,) * 4,
        check_vma=False,
    )
```

```python
import functools

import jax
import jax.numpy as jnp
from jax import lax
from jax.experimental import pallas as pl
from jax.experimental.pallas import tpu as pltpu
from jax.sharding import PartitionSpec as P

GROUP = 256
EPSILON = 1e-06
CHUNK = 4
MESH = pl.DeviceIdType.MESH
F32 = jnp.float32
BF16 = jnp.bfloat16
KK, VV = range(2)
QQ, GG = range(2)


def dot(a, b, ca=1, cb=0):
    return lax.dot_general(a, b, (((ca,), (cb,)), ((), ())), preferred_element_type=F32)


def flag(cond):
    return jnp.where(cond, 1.0, 0.0).astype(F32)


def doc_ends(doc_ref):
    ends, total = [], 0
    for j in range(doc_ref.shape[0]):
        total = total + doc_ref[j]
        ends.append(total)
    return ends


def seg_of(ends, p):
    s = (ends[0] <= p).astype(jnp.int32)
    for e in ends[1:]:
        s = s + (e <= p).astype(jnp.int32)
    return s


def last_end(ends, p):
    s = jnp.where(ends[0] <= p, ends[0], 0)
    for e in ends[1:]:
        s = jnp.where(e <= p, e, s)
    return s


def next_end(ends, p):
    s = ends[-1]
    for e in ends[-2::-1]:
        s = jnp.where(e > p, e, s)
    return s


def lane_gate(lower, limit):
    lane = lax.broadcasted_iota(jnp.int32, (16, GROUP), 1)
    one = jnp.where(lane >= limit if lower else lane < limit, 1.0, 0.0).astype(BF16)
    return jnp.concatenate([one] * 8, axis=0)


def far_first(n, per_chip):
    chips = n // per_chip

    def hops(d):
        c = d // per_chip
        return min(c, chips - c)

    return sorted(range(1, n), key=lambda d: -hops(d))


def main_kernel(
    sizes,
    doc_hbm,
    q_hbm,
    k_hbm,
    v_hbm,
    g_hbm,
    out_v,
    dq_v,
    dk_part,
    dv_part,
    k_after,
    v_after,
    weight,
    r_loc,
    r_in,
    raw,
    tmp,
    k_n,
    v_n,
    k_t,
    v_t,
    q_t,
    g_t,
    mask_ref,
    p_t,
    dp_t,
    o_t,
    dob_t,
    stage,
    s_loc,
    s_bf,
    keep_ref,
    doc_ref,
    s_got,
    s_pre,
    s_in,
    r_got,
    r_pre,
    part,
    t_got,
    scale_a,
    scale_b,
    in_sem,
    s_send,
    s_recv,
    t_send,
    t_recv,
    r_send,
    r_recv,
    u_send,
    u_recv,
    a_send,
    a_recv,
    doc_sem,
):
    n_seq, n_x, n_y, n_groups, n_heads = sizes
    tokens = n_groups * GROUP
    n_head = n_x * n_y
    width_all = float(n_head * n_heads * 128)
    n_chunks = n_groups // CHUNK
    me = lax.axis_index("seq")
    head = lax.axis_index("head")
    mx = lax.rem(head, n_x)
    my = head // n_x
    slab = 128 // n_seq
    seq_order = far_first(n_seq, 2)
    head_order = sorted(
        range(1, n_head),
        key=lambda d: -(min(d % n_x, n_x - d % n_x) + min(d // n_x, n_y - d // n_x)),
    )

    def seq_peer(d):
        return lax.rem(me + d, n_seq)

    def head_peer(d, sign):
        x = lax.rem(mx + n_x + sign * (d % n_x), n_x)
        y = lax.rem(my + n_y + sign * (d // n_x), n_y)
        return y * n_x + x

    doc_copy = pltpu.make_async_copy(doc_hbm, doc_ref, doc_sem)
    doc_copy.start()
    sources = (k_hbm, v_hbm, q_hbm, g_hbm)

    def load(a, g):
        return pltpu.make_async_copy(sources[a].at[g], raw.at[a, g], in_sem.at[a, g])

    @pl.loop(0, n_groups)
    def _(g):
        load(0, g).start()
        load(1, g).start()

    @pl.loop(0, n_groups)
    def _(g):
        load(2, g).start()
        load(3, g).start()

    barrier = pltpu.get_barrier_semaphore()
    for d in seq_order:
        pl.semaphore_signal(barrier, inc=1, device_id={"seq": seq_peer(d)}, device_id_type=MESH)
    for d in head_order:
        pl.semaphore_signal(barrier, inc=1, device_id={"head": head_peer(d, 1)}, device_id_type=MESH)

    doc_copy.wait()
    ends = doc_ends(doc_ref)
    shard_first = me * tokens
    after_s = seg_of(ends, shard_first + tokens)
    bs = seg_of(ends, shard_first - 1)

    def edges(g):
        first = shard_first + g * GROUP
        return (
            seg_of(ends, first - 1),
            seg_of(ends, first),
            seg_of(ends, first + GROUP - 1),
            seg_of(ends, first + GROUP),
        )

    def before_gate(g):
        first = shard_first + g * GROUP
        return lane_gate(False, next_end(ends, first - 1) - first)

    def tail_gate(g):
        first = shard_first + g * GROUP
        return lane_gate(True, last_end(ends, first + GROUP - 1) - first)

    def lead_gate(g):
        first = shard_first + g * GROUP
        return lane_gate(False, next_end(ends, first) - first)

    both_heads = range(n_heads)

    def spread(a, g, slot):
        tmp[slot] = raw[a, g].astype(F32)
        return [tmp[slot, pl.ds(h, GROUP, stride=n_heads), :].astype(BF16) for h in both_heads]

    def join(slot, parts):
        for h in both_heads:
            stage[slot, pl.ds(h, GROUP, stride=n_heads), :] = parts[h].astype(BF16).T.astype(F32)
        return stage[slot].astype(BF16)

    def put(ref, g, parts):
        for h in both_heads:
            ref[g, pl.ds(h, GROUP, stride=n_heads), :] = parts[h].astype(F32).T

    def key_states(groups, h):
        added = [dot(v_t[h, g] * tail_gate(g), k_n[h, g]) for g in groups]
        for g, new in zip(groups, added):
            bc, c0, c1, ac = edges(g)
            s_loc[h, g + 1] = flag(c1 == bc) * s_loc[h, g] + new

    def hand(src, dst, send, recv, d):
        return pltpu.make_async_remote_copy(
            src_ref=src,
            dst_ref=dst,
            send_sem=send,
            recv_sem=recv,
            device_id={"seq": seq_peer(d)},
            device_id_type=MESH,
        )

    def everything(got, h, send, recv):
        return hand(got.at[h, pl.ds(0, n_seq - 1)], got.at[h, pl.ds(0, n_seq - 1)], send, recv, 1)

    def rows(ref, h, i):
        return ref.at[h, pl.ds(pl.multiple_of(i * slab, slab), slab)]

    class Run:
        def __init__(self, ref, slot):
            self.ref, self.slot = ref, slot

        @property
        def at(self):
            return self

        def __getitem__(self, index):
            h, rest = index
            return self.ref.at[h, self.slot, rest]

    s_run, r_run = Run(s_loc, n_groups), Run(r_loc, 0)

    def scatter(h, run, got, send, recv):
        for d in seq_order:
            hand(rows(run, h, seq_peer(d)), got.at[h, me], send.at[h], recv.at[h], d).start()

    def combine(h, run, got, pre, into, send, recv, backward):
        mine = pl.ds(pl.multiple_of(me * slab, slab), slab)
        got[h, me] = run.ref[h, run.slot, mine, :]
        everything(got, h, send.at[h], recv.at[h]).wait_recv()
        carry = jnp.zeros((slab, 128), F32)
        for i in range(n_seq - 1, -1, -1) if backward else range(n_seq):
            pre[h, i] = carry
            carry = keep_ref[1 if backward else 0, i] * carry + got[h, i]
        into[h, mine, :] = pre[h, me]

    def give(h, pre, into, send, recv):
        for d in seq_order:
            hand(pre.at[h, seq_peer(d)], rows(into, h, me), send.at[h], recv.at[h], d).start()

    def give_done(h, got, send, recv):
        everything(got, h, send.at[h], recv.at[h]).wait_recv()

    def sends_done(h, got, *pairs):
        for send, recv in pairs:
            everything(got, h, send.at[h], recv.at[h]).wait_send()

    pair = 2
    for h in both_heads:
        s_loc[h, 0] = jnp.zeros((128, 128), F32)

    @pl.loop(0, n_groups // pair)
    def _(i):
        groups = [i * pair + u for u in range(pair)]
        for g in groups:
            load(0, g).wait()
            load(1, g).wait()
        for u, g in enumerate(groups):
            for h, x in enumerate(spread(0, g, 2 * u)):
                k_n[h, g] = x
            for h, x in enumerate(spread(1, g, 2 * u + 1)):
                v_n[h, g] = x
                v_t[h, g] = x.T
        key_states(groups, 0)

    pl.semaphore_wait(barrier, n_seq - 1 + n_head - 1)
    scatter(0, s_run, s_got, s_send, s_recv)

    for h in range(1, n_heads):

        @pl.loop(0, n_groups // CHUNK)
        def _(i):
            key_states([i * CHUNK + u for u in range(CHUNK)], h)

        scatter(h, s_run, s_got, s_send, s_recv)

    for i in range(n_seq):
        first = i * tokens
        keep_ref[0, i] = flag(seg_of(ends, first + tokens - 1) == seg_of(ends, first - 1))
        keep_ref[1, i] = flag(seg_of(ends, first) == seg_of(ends, first + tokens))

    def build_mask(g):
        first = shard_first + g * GROUP
        lane8 = lax.broadcasted_iota(jnp.int32, (8, GROUP), 1)
        start = jnp.broadcast_to((last_end(ends, lane8 + first) - first)[0:1], (GROUP, GROUP))
        key = lax.broadcasted_iota(jnp.int32, (GROUP, GROUP), 0)
        query = lax.broadcasted_iota(jnp.int32, (GROUP, GROUP), 1)
        mask_ref[g] = jnp.where(jnp.logical_and(key >= start, key <= query), 1.0, 0.0).astype(F32)

    def intra(i):
        groups = [i * pair + u for u in range(pair)]
        for u, g in enumerate(groups):
            load(2, g).wait()
            build_mask(g)
            for h, x in enumerate(spread(2, g, u)):
                q_t[h, g] = x.T
                k_t[h, g] = k_n[h, g].T
        for g in groups:
            for h in both_heads:
                p_t[h, g] = (dot(k_n[h, g], q_t[h, g]) * mask_ref[g]).astype(BF16)
        for g in groups:
            for h in both_heads:
                o_t[h, g] = dot(v_t[h, g], p_t[h, g])

    n_pairs = n_groups // pair
    cut1, cut2 = (2 * n_pairs) // 3, (5 * n_pairs) // 6

    @pl.loop(0, cut1)
    def _(i):
        intra(i)

    combine(0, s_run, s_got, s_pre, s_in, s_send, s_recv, False)
    give(0, s_pre, s_in, t_send, t_recv)

    @pl.loop(cut1, cut2)
    def _(i):
        intra(i)

    for h in range(1, n_heads):
        combine(h, s_run, s_got, s_pre, s_in, s_send, s_recv, False)
        give(h, s_pre, s_in, t_send, t_recv)

    @pl.loop(cut2, n_pairs)
    def _(i):
        intra(i)

    @pl.loop(0, n_pairs)
    def _(i):
        groups = [i * pair + u for u in range(pair)]
        for u, g in enumerate(groups):
            load(3, g).wait()
            for h, x in enumerate(spread(3, g, u)):
                g_t[h, g] = x.T

    def outer(groups, h):
        for g in groups:
            bc, c0, c1, ac = edges(g)
            s_bf[h, g] = (s_loc[h, g] + flag(bc == bs) * s_in[h]).astype(BF16)
        more = [dot(s_bf[h, g], q_t[h, g] * before_gate(g)) for g in groups]
        for g, x in zip(groups, more):
            o = o_t[h, g] + x
            o_t[h, g] = o
            c, r = g // CHUNK, lax.rem(g, CHUNK)
            squares = jnp.sum(o * o, axis=0, keepdims=True)
            inner = jnp.sum(g_t[h, g].astype(F32) * o, axis=0, keepdims=True)
            one, two = pl.ds(r, 1), pl.ds(CHUNK + r, 1)
            if h == 0:
                part[c, one, :] = squares
                part[c, two, :] = inner
            else:
                part[c, one, :] += squares
                part[c, two, :] += inner

    for h in range(n_heads - 1):
        give_done(h, s_pre, t_send, t_recv)

        @pl.loop(0, n_pairs)
        def _(i):
            outer([i * pair + u for u in range(pair)], h)

    give_done(n_heads - 1, s_pre, t_send, t_recv)

    def part_copy(c, d):
        return pltpu.make_async_remote_copy(
            src_ref=part.at[c],
            dst_ref=t_got.at[c, head],
            send_sem=a_send.at[c],
            recv_sem=a_recv.at[c],
            device_id={"head": head_peer(d, 1)},
            device_id_type=MESH,
        )

    def all_parts(c):
        return pltpu.make_async_remote_copy(
            src_ref=t_got.at[c, pl.ds(0, n_head - 1)],
            dst_ref=t_got.at[c, pl.ds(0, n_head - 1)],
            send_sem=a_send.at[c],
            recv_sem=a_recv.at[c],
            device_id={"head": head_peer(1, 1)},
            device_id_type=MESH,
        )

    for c in range(n_chunks - 1, -1, -1):

        @pl.loop(0, CHUNK // pair)
        def _(i):
            outer([c * CHUNK + i * pair + u for u in range(pair)], n_heads - 1)

        for d in head_order:
            part_copy(c, d).start()
        t_got[c, head] = part[c]

    for h in both_heads:
        r_loc[h, n_groups] = jnp.zeros((128, 128), F32)

    def wide(ref, g):
        c, r = g // CHUNK, lax.rem(g, CHUNK)
        return jnp.broadcast_to(ref[c, pl.ds(r, 1), :], (128, GROUP))

    def back_states(groups, heads):
        for g in groups:
            for h in heads:
                dob_t[h, g] = (g_t[h, g].astype(F32) * wide(scale_a, g) - o_t[h, g] * wide(scale_b, g)).astype(BF16)
        added = [[dot(q_t[h, g] * lead_gate(g), dob_t[h, g], 1, 1) for h in heads] for g in groups]
        for g, row in zip(groups, added):
            bc, c0, c1, ac = edges(g)
            for h, new in zip(heads, row):
                r_loc[h, g] = flag(c0 == ac) * r_loc[h, g + 1] + new

    def gather_part(c):
        all_parts(c).wait_recv()
        value = t_got[c, 0]
        for i in range(1, n_head):
            value = value + t_got[c, i]
        a = 1.0 / jnp.sqrt(value[:CHUNK] / width_all + EPSILON)
        scale_a[c, 0:CHUNK] = a
        scale_b[c, 0:CHUNK] = a * a * (a * value[CHUNK:] / width_all)

    for c in range(n_chunks - 1, 0, -1):
        gather_part(c)

        @pl.loop(0, CHUNK // pair)
        def _(i):
            top = c * CHUNK + CHUNK - 1 - i * pair
            back_states([top - u for u in range(pair)], both_heads)

    gather_part(0)
    for h in both_heads:

        @pl.loop(0, CHUNK // pair)
        def _(i):
            top = CHUNK - 1 - i * pair
            back_states([top - u for u in range(pair)], [h])

        scatter(h, r_run, r_got, r_send, r_recv)

    def inner_back(g):
        before = before_gate(g)
        bc, c0, c1, ac = edges(g)
        weight[g] = jnp.broadcast_to(flag(ac == after_s), (8, 128))
        first = shard_first + g * GROUP
        row = lax.broadcasted_iota(jnp.int32, (GROUP, 128), 0)
        after = jnp.where(row >= last_end(ends, first + GROUP) - first, 1.0, 0.0).astype(BF16)
        for h in both_heads:
            dp_t[h] = (dot(v_n[h, g], dob_t[h, g]) * mask_ref[g]).astype(BF16)
        put(dv_part, g, [dot(dob_t[h, g], p_t[h, g], 1, 1) for h in both_heads])
        out_v[g] = join(0, [o_t[h, g] * wide(scale_a, g) for h in both_heads])
        more = [dot(s_bf[h, g], dob_t[h, g] * before, 0, 0) for h in both_heads]
        dq_v[g] = join(1, [dot(k_t[h, g], dp_t[h]) + more[h] for h in both_heads])
        put(dk_part, g, [dot(q_t[h, g], dp_t[h], 1, 1) for h in both_heads])
        for h in both_heads:
            k_after[h, g] = k_n[h, g] * after
            v_after[h, g] = v_n[h, g] * after

    cut1, cut2 = (2 * n_groups) // 3, (5 * n_groups) // 6

    @pl.loop(0, cut1)
    def _(g):
        inner_back(g)

    combine(0, r_run, r_got, r_pre, r_in, r_send, r_recv, True)
    give(0, r_pre, r_in, u_send, u_recv)

    @pl.loop(cut1, cut2)
    def _(g):
        inner_back(g)

    for h in range(1, n_heads):
        combine(h, r_run, r_got, r_pre, r_in, r_send, r_recv, True)
        give(h, r_pre, r_in, u_send, u_recv)

    @pl.loop(cut2, n_groups)
    def _(g):
        inner_back(g)

    for h in both_heads:
        sends_done(h, s_pre, (s_send, s_recv), (t_send, t_recv), (r_send, r_recv))
    for c in range(n_chunks):
        all_parts(c).wait_send()
    for h in both_heads:
        give_done(h, r_pre, u_send, u_recv)
        sends_done(h, r_pre, (u_send, u_recv))


def last_kernel(
    sizes,
    out_v,
    dq_v,
    dk_part,
    dv_part,
    k_after,
    v_after,
    weight,
    r_loc,
    r_in,
    out_hbm,
    dq_hbm,
    dk_hbm,
    dv_hbm,
    stage,
    done,
    sem,
    whole,
):
    n_seq, n_x, n_y, n_groups, n_heads = sizes
    copies = [
        pltpu.make_async_copy(out_v, out_hbm, whole.at[0]),
        pltpu.make_async_copy(dq_v, dq_hbm, whole.at[1]),
    ]
    for c in copies:
        c.start()
    targets = (dk_hbm, dv_hbm)
    parts = (dk_part, dv_part)
    batch = 4

    def store(i, g):
        return pltpu.make_async_copy(done.at[i, g], targets[i].at[g], sem.at[i, g])

    @pl.loop(0, n_groups // batch)
    def _(step):
        for u in range(batch):
            g = step * batch + u
            w = jnp.broadcast_to(weight[g, 0:1, :], (128, 128))
            for h in range(n_heads):
                state = (r_loc[h, g + 1] + w * r_in[h]).astype(BF16)
                even = pl.ds(h, GROUP, stride=n_heads)
                stage[2 * u, even, :] = dot(v_after[h, g], state, 1, 1)
                stage[2 * u + 1, even, :] = dot(k_after[h, g], state)
            for i in range(2):
                done[i, g] = (stage[2 * u + i] + parts[i][g]).astype(BF16)
                store(i, g).start()

    @pl.loop(0, n_groups)
    def _(g):
        for i in range(2):
            store(i, g).wait()

    for c in copies:
        c.wait()


def per_device(sizes, queries, keys, values, cotangent, doc_lengths):
    tokens_here, n_heads, width = queries.shape
    n_seq, n_x, n_y = sizes
    n_groups = tokens_here // GROUP
    n_chunks = n_groups // CHUNK
    rows2 = GROUP * n_heads
    slab = width // n_seq
    sizes = (n_seq, n_x, n_y, n_groups, n_heads)
    view = lambda x: x.reshape(n_groups, rows2, width)
    dma = pltpu.SemaphoreType.DMA
    vm = pltpu.VMEM
    anywhere = pl.BlockSpec(memory_space=pl.ANY)
    on_chip = pl.BlockSpec(memory_space=pltpu.VMEM)
    per_head = (n_heads, n_groups, GROUP, width)
    turned = (n_heads, n_groups, width, GROUP)
    states = (n_heads, n_groups + 1, width, width)
    one_state = (n_heads, width, width)
    slices = (n_heads, n_seq, slab, width)
    sums = (n_chunks, 2 * CHUNK, GROUP)
    packed = (n_groups, rows2, width)
    mids = pl.pallas_call(
        functools.partial(main_kernel, sizes),
        out_shape=(
            vm(packed, BF16),
            vm(packed, BF16),
            vm(packed, F32),
            vm(packed, F32),
            vm(per_head, BF16),
            vm(per_head, BF16),
            vm((n_groups, 8, 128), F32),
            vm(states, F32),
            vm(one_state, F32),
        ),
        in_specs=[anywhere] * 5,
        out_specs=(on_chip,) * 9,
        scratch_shapes=[
            vm((4,) + packed, BF16),
            vm((4, rows2, width), F32),
            vm(per_head, BF16),
            vm(per_head, BF16),
            vm(turned, BF16),
            vm(turned, BF16),
            vm(turned, BF16),
            vm(turned, BF16),
            vm((n_groups, GROUP, GROUP), F32),
            vm((n_heads, n_groups, GROUP, GROUP), BF16),
            vm((n_heads, GROUP, GROUP), BF16),
            vm(turned, F32),
            vm(turned, BF16),
            vm((2, rows2, width), F32),
            vm(states, F32),
            vm((n_heads, n_groups, width, width), BF16),
            pltpu.SMEM((2, n_seq), F32),
            pltpu.SMEM(doc_lengths.shape, jnp.int32),
            vm(slices, F32),
            vm(slices, F32),
            vm(one_state, F32),
            vm(slices, F32),
            vm(slices, F32),
            vm(sums, F32),
            vm((n_chunks, n_x * n_y, 2 * CHUNK, GROUP), F32),
            vm(sums, F32),
            vm(sums, F32),
            dma((4, n_groups)),
        ]
        + [dma((n_heads,))] * 8
        + [dma((n_chunks,))] * 2
        + [dma],
        compiler_params=pltpu.CompilerParams(
            collective_id=0, has_side_effects=True, vmem_limit_bytes=44 << 20
        ),
        name="exchange_and_attend",
    )(doc_lengths, view(queries), view(keys), view(values), view(cotangent))
    mids = [pltpu.with_memory_space_constraint(m, pltpu.VMEM) for m in mids]
    results = pl.pallas_call(
        functools.partial(last_kernel, sizes),
        out_shape=(jax.ShapeDtypeStruct(packed, BF16),) * 4,
        in_specs=[on_chip] * 9,
        out_specs=(anywhere,) * 4,
        scratch_shapes=[
            vm((8, rows2, width), F32),
            vm((2,) + packed, BF16),
            dma((2, n_groups)),
            dma((2,)),
        ],
        compiler_params=pltpu.CompilerParams(vmem_limit_bytes=16 << 20),
        name="finish",
    )(*mids)
    return tuple(r.reshape(tokens_here, n_heads, width) for r in results)


def solution(mesh):
    n_x = 4
    spec = P("seq", "head", None)
    return jax.shard_map(
        functools.partial(per_device, (mesh.shape["seq"], n_x, mesh.shape["head"] // n_x)),
        mesh=mesh,
        in_specs=(spec,) * 4 + (P(),),
        out_specs=(spec,) * 4,
        check_vma=False,
    )
```

```python
import functools

import jax
import jax.numpy as jnp
from jax import lax
from jax.experimental import pallas as pl
from jax.experimental.pallas import tpu as pltpu
from jax.sharding import PartitionSpec as P

GROUP = 256
EPSILON = 1e-06
CHUNK = 4
MESH = pl.DeviceIdType.MESH
F32 = jnp.float32
BF16 = jnp.bfloat16
KK, VV = range(2)
QQ, GG = range(2)


def dot(a, b, ca=1, cb=0):
    return lax.dot_general(a, b, (((ca,), (cb,)), ((), ())), preferred_element_type=F32)


def flag(cond):
    return jnp.where(cond, 1.0, 0.0).astype(F32)


def doc_ends(doc_ref):
    ends, total = [], 0
    for j in range(doc_ref.shape[0]):
        total = total + doc_ref[j]
        ends.append(total)
    return ends


def seg_of(ends, p):
    s = (ends[0] <= p).astype(jnp.int32)
    for e in ends[1:]:
        s = s + (e <= p).astype(jnp.int32)
    return s


def last_end(ends, p):
    s = jnp.where(ends[0] <= p, ends[0], 0)
    for e in ends[1:]:
        s = jnp.where(e <= p, e, s)
    return s


def next_end(ends, p):
    s = ends[-1]
    for e in ends[-2::-1]:
        s = jnp.where(e > p, e, s)
    return s


def lane_gate(lower, limit):
    lane = lax.broadcasted_iota(jnp.int32, (16, GROUP), 1)
    one = jnp.where(lane >= limit if lower else lane < limit, 1.0, 0.0).astype(BF16)
    return jnp.concatenate([one] * 8, axis=0)


def far_first(n, per_chip):
    chips = n // per_chip

    def hops(d):
        c = d // per_chip
        return min(c, chips - c)

    return sorted(range(1, n), key=lambda d: -hops(d))


def main_kernel(
    sizes,
    doc_hbm,
    q_hbm,
    k_hbm,
    v_hbm,
    g_hbm,
    out_v,
    dq_v,
    dk_part,
    dv_part,
    k_after,
    v_after,
    weight,
    r_loc,
    r_in,
    raw,
    tmp,
    k_n,
    v_n,
    k_t,
    v_t,
    q_t,
    g_t,
    mask_ref,
    p_t,
    dp_t,
    o_t,
    dob_t,
    stage,
    s_loc,
    s_bf,
    keep_ref,
    doc_ref,
    s_got,
    s_pre,
    s_in,
    r_got,
    r_pre,
    part,
    t_got,
    scale_a,
    scale_b,
    in_sem,
    s_send,
    s_recv,
    t_send,
    t_recv,
    r_send,
    r_recv,
    u_send,
    u_recv,
    a_send,
    a_recv,
    doc_sem,
):
    n_seq, n_x, n_y, n_groups, n_heads = sizes
    tokens = n_groups * GROUP
    n_head = n_x * n_y
    width_all = float(n_head * n_heads * 128)
    n_chunks = n_groups // CHUNK
    me = lax.axis_index("seq")
    head = lax.axis_index("head")
    mx = lax.rem(head, n_x)
    my = head // n_x
    slab = 128 // n_seq
    seq_order = far_first(n_seq, 2)
    head_order = sorted(
        range(1, n_head),
        key=lambda d: -(min(d % n_x, n_x - d % n_x) + min(d // n_x, n_y - d // n_x)),
    )

    def seq_peer(d):
        return lax.rem(me + d, n_seq)

    def head_peer(d, sign):
        x = lax.rem(mx + n_x + sign * (d % n_x), n_x)
        y = lax.rem(my + n_y + sign * (d // n_x), n_y)
        return y * n_x + x

    doc_copy = pltpu.make_async_copy(doc_hbm, doc_ref, doc_sem)
    doc_copy.start()
    sources = (k_hbm, v_hbm, q_hbm, g_hbm)

    pair = 2

    def load(a, g):
        two = pl.ds(g, pair)
        return pltpu.make_async_copy(sources[a].at[two], raw.at[a, two], in_sem.at[a, g // pair])

    @pl.loop(0, n_groups // pair)
    def _(i):
        load(0, i * pair).start()
        load(1, i * pair).start()

    @pl.loop(0, n_groups // pair)
    def _(i):
        load(2, i * pair).start()
        load(3, i * pair).start()

    barrier = pltpu.get_barrier_semaphore()
    for d in seq_order:
        pl.semaphore_signal(barrier, inc=1, device_id={"seq": seq_peer(d)}, device_id_type=MESH)
    for d in head_order:
        pl.semaphore_signal(barrier, inc=1, device_id={"head": head_peer(d, 1)}, device_id_type=MESH)

    doc_copy.wait()
    ends = doc_ends(doc_ref)
    shard_first = me * tokens
    after_s = seg_of(ends, shard_first + tokens)
    bs = seg_of(ends, shard_first - 1)

    def edges(g):
        first = shard_first + g * GROUP
        return (
            seg_of(ends, first - 1),
            seg_of(ends, first),
            seg_of(ends, first + GROUP - 1),
            seg_of(ends, first + GROUP),
        )

    def before_gate(g):
        first = shard_first + g * GROUP
        return lane_gate(False, next_end(ends, first - 1) - first)

    def tail_gate(g):
        first = shard_first + g * GROUP
        return lane_gate(True, last_end(ends, first + GROUP - 1) - first)

    def lead_gate(g):
        first = shard_first + g * GROUP
        return lane_gate(False, next_end(ends, first) - first)

    both_heads = range(n_heads)

    def spread(a, g, slot):
        tmp[slot] = raw[a, g].astype(F32)
        return [tmp[slot, pl.ds(h, GROUP, stride=n_heads), :].astype(BF16) for h in both_heads]

    def join(slot, parts):
        for h in both_heads:
            stage[slot, pl.ds(h, GROUP, stride=n_heads), :] = parts[h].astype(BF16).T.astype(F32)
        return stage[slot].astype(BF16)

    def put(ref, g, parts):
        for h in both_heads:
            ref[g, pl.ds(h, GROUP, stride=n_heads), :] = parts[h].astype(F32).T

    def key_states(groups, h):
        added = [dot(v_t[h, g] * tail_gate(g), k_n[h, g]) for g in groups]
        for g, new in zip(groups, added):
            bc, c0, c1, ac = edges(g)
            s_loc[h, g + 1] = flag(c1 == bc) * s_loc[h, g] + new

    def hand(src, dst, send, recv, d):
        return pltpu.make_async_remote_copy(
            src_ref=src,
            dst_ref=dst,
            send_sem=send,
            recv_sem=recv,
            device_id={"seq": seq_peer(d)},
            device_id_type=MESH,
        )

    def everything(got, h, send, recv):
        return hand(got.at[h, pl.ds(0, n_seq - 1)], got.at[h, pl.ds(0, n_seq - 1)], send, recv, 1)

    def rows(ref, h, i):
        return ref.at[h, pl.ds(pl.multiple_of(i * slab, slab), slab)]

    class Run:
        def __init__(self, ref, slot):
            self.ref, self.slot = ref, slot

        @property
        def at(self):
            return self

        def __getitem__(self, index):
            h, rest = index
            return self.ref.at[h, self.slot, rest]

    s_run, r_run = Run(s_loc, n_groups), Run(r_loc, 0)

    def scatter(h, run, got, send, recv):
        for d in seq_order:
            hand(rows(run, h, seq_peer(d)), got.at[h, me], send.at[h], recv.at[h], d).start()

    def combine(h, run, got, pre, into, send, recv, backward):
        mine = pl.ds(pl.multiple_of(me * slab, slab), slab)
        got[h, me] = run.ref[h, run.slot, mine, :]
        everything(got, h, send.at[h], recv.at[h]).wait_recv()
        carry = jnp.zeros((slab, 128), F32)
        for i in range(n_seq - 1, -1, -1) if backward else range(n_seq):
            pre[h, i] = carry
            carry = keep_ref[1 if backward else 0, i] * carry + got[h, i]
        into[h, mine, :] = pre[h, me]

    def give(h, pre, into, send, recv):
        for d in seq_order:
            hand(pre.at[h, seq_peer(d)], rows(into, h, me), send.at[h], recv.at[h], d).start()

    def give_done(h, got, send, recv):
        everything(got, h, send.at[h], recv.at[h]).wait_recv()

    def sends_done(h, got, *pairs):
        for send, recv in pairs:
            everything(got, h, send.at[h], recv.at[h]).wait_send()

    for h in both_heads:
        s_loc[h, 0] = jnp.zeros((128, 128), F32)

    def batch(i):
        return [i * CHUNK + u for u in range(CHUNK)]

    def take_keys_values(groups):
        for half in range(CHUNK // pair):
            load(0, groups[half * pair]).wait()
            load(1, groups[half * pair]).wait()
        for u, g in enumerate(groups):
            for h, x in enumerate(spread(1, g, 2 * u + 1)):
                v_n[h, g] = x
                v_t[h, g] = x.T
            for h, x in enumerate(spread(0, g, 2 * u)):
                k_n[h, g] = x

    @pl.loop(0, n_groups // CHUNK)
    def _(i):
        take_keys_values(batch(i))
        key_states(batch(i), 0)

    pl.semaphore_wait(barrier, n_seq - 1 + n_head - 1)
    scatter(0, s_run, s_got, s_send, s_recv)

    for h in range(1, n_heads):

        @pl.loop(0, n_groups // CHUNK)
        def _(i):
            key_states(batch(i), h)

        scatter(h, s_run, s_got, s_send, s_recv)

    for i in range(n_seq):
        first = i * tokens
        keep_ref[0, i] = flag(seg_of(ends, first + tokens - 1) == seg_of(ends, first - 1))
        keep_ref[1, i] = flag(seg_of(ends, first) == seg_of(ends, first + tokens))

    def build_mask(g):
        first = shard_first + g * GROUP
        lane8 = lax.broadcasted_iota(jnp.int32, (8, GROUP), 1)
        start = jnp.broadcast_to((last_end(ends, lane8 + first) - first)[0:1], (GROUP, GROUP))
        key = lax.broadcasted_iota(jnp.int32, (GROUP, GROUP), 0)
        query = lax.broadcasted_iota(jnp.int32, (GROUP, GROUP), 1)
        mask_ref[g] = jnp.where(jnp.logical_and(key >= start, key <= query), 1.0, 0.0).astype(F32)

    def intra(i):
        groups = [i * pair + u for u in range(pair)]
        load(2, groups[0]).wait()
        for u, g in enumerate(groups):
            build_mask(g)
            for h, x in enumerate(spread(2, g, u)):
                q_t[h, g] = x.T
                k_t[h, g] = k_n[h, g].T
        for g in groups:
            for h in both_heads:
                p_t[h, g] = (dot(k_n[h, g], q_t[h, g]) * mask_ref[g]).astype(BF16)
        for g in groups:
            for h in both_heads:
                o_t[h, g] = dot(v_t[h, g], p_t[h, g])

    n_pairs = n_groups // pair

    def take_cotangent(groups):
        for half in range(CHUNK // pair):
            load(3, groups[half * pair]).wait()
        for u, g in enumerate(groups):
            for h, x in enumerate(spread(3, g, u)):
                g_t[h, g] = x.T

    @pl.loop(0, n_pairs - 1)
    def _(i):
        intra(i)

    for h in both_heads:
        combine(h, s_run, s_got, s_pre, s_in, s_send, s_recv, False)
        give(h, s_pre, s_in, t_send, t_recv)
        if h == 0:
            take_cotangent(batch(0))

    intra(n_pairs - 1)

    @pl.loop(1, n_groups // CHUNK)
    def _(i):
        take_cotangent(batch(i))

    def outer(groups, h):
        for g in groups:
            bc, c0, c1, ac = edges(g)
            s_bf[h, g] = (s_loc[h, g] + flag(bc == bs) * s_in[h]).astype(BF16)
        more = [dot(s_bf[h, g], q_t[h, g] * before_gate(g)) for g in groups]
        for g, x in zip(groups, more):
            o = o_t[h, g] + x
            o_t[h, g] = o
            c, r = g // CHUNK, lax.rem(g, CHUNK)
            squares = jnp.sum(o * o, axis=0, keepdims=True)
            inner = jnp.sum(g_t[h, g].astype(F32) * o, axis=0, keepdims=True)
            one, two = pl.ds(r, 1), pl.ds(CHUNK + r, 1)
            if h == 0:
                part[c, one, :] = squares
                part[c, two, :] = inner
            else:
                part[c, one, :] += squares
                part[c, two, :] += inner

    for h in range(n_heads - 1):
        give_done(h, s_pre, t_send, t_recv)

        @pl.loop(0, n_groups // CHUNK)
        def _(i):
            outer([i * CHUNK + u for u in range(CHUNK)], h)

    give_done(n_heads - 1, s_pre, t_send, t_recv)

    def part_copy(c, d):
        return pltpu.make_async_remote_copy(
            src_ref=part.at[c],
            dst_ref=t_got.at[c, head],
            send_sem=a_send.at[c],
            recv_sem=a_recv.at[c],
            device_id={"head": head_peer(d, 1)},
            device_id_type=MESH,
        )

    def all_parts(c):
        return pltpu.make_async_remote_copy(
            src_ref=t_got.at[c, pl.ds(0, n_head - 1)],
            dst_ref=t_got.at[c, pl.ds(0, n_head - 1)],
            send_sem=a_send.at[c],
            recv_sem=a_recv.at[c],
            device_id={"head": head_peer(1, 1)},
            device_id_type=MESH,
        )

    for c in range(n_chunks - 1, -1, -1):

        outer([c * CHUNK + u for u in range(CHUNK)], n_heads - 1)

        for d in head_order:
            part_copy(c, d).start()
        t_got[c, head] = part[c]

    for h in both_heads:
        r_loc[h, n_groups] = jnp.zeros((128, 128), F32)

    def wide(ref, g):
        c, r = g // CHUNK, lax.rem(g, CHUNK)
        return jnp.broadcast_to(ref[c, pl.ds(r, 1), :], (128, GROUP))

    def back_states(groups, heads):
        for g in groups:
            for h in heads:
                dob_t[h, g] = (g_t[h, g].astype(F32) * wide(scale_a, g) - o_t[h, g] * wide(scale_b, g)).astype(BF16)
        added = [[dot(q_t[h, g] * lead_gate(g), dob_t[h, g], 1, 1) for h in heads] for g in groups]
        for g, row in zip(groups, added):
            bc, c0, c1, ac = edges(g)
            for h, new in zip(heads, row):
                r_loc[h, g] = flag(c0 == ac) * r_loc[h, g + 1] + new

    def gather_part(c):
        all_parts(c).wait_recv()
        value = t_got[c, 0]
        for i in range(1, n_head):
            value = value + t_got[c, i]
        a = 1.0 / jnp.sqrt(value[:CHUNK] / width_all + EPSILON)
        scale_a[c, 0:CHUNK] = a
        scale_b[c, 0:CHUNK] = a * a * (a * value[CHUNK:] / width_all)

    for c in range(n_chunks - 1, 0, -1):
        gather_part(c)

        back_states([c * CHUNK + CHUNK - 1 - u for u in range(CHUNK)], both_heads)

    gather_part(0)
    for h in both_heads:

        back_states([CHUNK - 1 - u for u in range(CHUNK)], [h])

        scatter(h, r_run, r_got, r_send, r_recv)

    def inner_back(g):
        before = before_gate(g)
        bc, c0, c1, ac = edges(g)
        weight[g] = jnp.broadcast_to(flag(ac == after_s), (8, 128))
        first = shard_first + g * GROUP
        row = lax.broadcasted_iota(jnp.int32, (GROUP, 128), 0)
        after = jnp.where(row >= last_end(ends, first + GROUP) - first, 1.0, 0.0).astype(BF16)
        for h in both_heads:
            dp_t[h] = (dot(v_n[h, g], dob_t[h, g]) * mask_ref[g]).astype(BF16)
        put(dv_part, g, [dot(dob_t[h, g], p_t[h, g], 1, 1) for h in both_heads])
        out_v[g] = join(0, [o_t[h, g] * wide(scale_a, g) for h in both_heads])
        more = [dot(s_bf[h, g], dob_t[h, g] * before, 0, 0) for h in both_heads]
        dq_v[g] = join(1, [dot(k_t[h, g], dp_t[h]) + more[h] for h in both_heads])
        put(dk_part, g, [dot(q_t[h, g], dp_t[h], 1, 1) for h in both_heads])
        for h in both_heads:
            k_after[h, g] = k_n[h, g] * after
            v_after[h, g] = v_n[h, g] * after

    cut1, cut2 = n_groups // 2, n_groups // 2 + 1

    @pl.loop(0, cut1)
    def _(g):
        inner_back(g)

    combine(0, r_run, r_got, r_pre, r_in, r_send, r_recv, True)
    give(0, r_pre, r_in, u_send, u_recv)

    @pl.loop(cut1, cut2)
    def _(g):
        inner_back(g)

    for h in range(1, n_heads):
        combine(h, r_run, r_got, r_pre, r_in, r_send, r_recv, True)
        give(h, r_pre, r_in, u_send, u_recv)

    @pl.loop(cut2, n_groups)
    def _(g):
        inner_back(g)

    for h in both_heads:
        sends_done(h, s_pre, (s_send, s_recv), (t_send, t_recv), (r_send, r_recv))
    for c in range(n_chunks):
        all_parts(c).wait_send()
    for h in both_heads:
        give_done(h, r_pre, u_send, u_recv)
        sends_done(h, r_pre, (u_send, u_recv))


def last_kernel(
    sizes,
    out_v,
    dq_v,
    dk_part,
    dv_part,
    k_after,
    v_after,
    weight,
    r_loc,
    r_in,
    out_hbm,
    dq_hbm,
    dk_hbm,
    dv_hbm,
    stage,
    done,
    sem,
    whole,
):
    n_seq, n_x, n_y, n_groups, n_heads = sizes
    copies = [
        pltpu.make_async_copy(out_v, out_hbm, whole.at[0]),
        pltpu.make_async_copy(dq_v, dq_hbm, whole.at[1]),
    ]
    for c in copies:
        c.start()
    targets = (dk_hbm, dv_hbm)
    parts = (dk_part, dv_part)
    batch = 4

    def store(i, g):
        return pltpu.make_async_copy(done.at[i, g], targets[i].at[g], sem.at[i, g])

    @pl.loop(0, n_groups // batch)
    def _(step):
        for u in range(batch):
            g = step * batch + u
            w = jnp.broadcast_to(weight[g, 0:1, :], (128, 128))
            for h in range(n_heads):
                state = (r_loc[h, g + 1] + w * r_in[h]).astype(BF16)
                even = pl.ds(h, GROUP, stride=n_heads)
                stage[2 * u, even, :] = dot(v_after[h, g], state, 1, 1)
                stage[2 * u + 1, even, :] = dot(k_after[h, g], state)
            for i in range(2):
                done[i, g] = (stage[2 * u + i] + parts[i][g]).astype(BF16)
                store(i, g).start()

    @pl.loop(0, n_groups)
    def _(g):
        for i in range(2):
            store(i, g).wait()

    for c in copies:
        c.wait()


def per_device(sizes, queries, keys, values, cotangent, doc_lengths):
    tokens_here, n_heads, width = queries.shape
    n_seq, n_x, n_y = sizes
    n_groups = tokens_here // GROUP
    n_chunks = n_groups // CHUNK
    rows2 = GROUP * n_heads
    slab = width // n_seq
    sizes = (n_seq, n_x, n_y, n_groups, n_heads)
    view = lambda x: x.reshape(n_groups, rows2, width)
    dma = pltpu.SemaphoreType.DMA
    vm = pltpu.VMEM
    anywhere = pl.BlockSpec(memory_space=pl.ANY)
    on_chip = pl.BlockSpec(memory_space=pltpu.VMEM)
    per_head = (n_heads, n_groups, GROUP, width)
    turned = (n_heads, n_groups, width, GROUP)
    states = (n_heads, n_groups + 1, width, width)
    one_state = (n_heads, width, width)
    slices = (n_heads, n_seq, slab, width)
    sums = (n_chunks, 2 * CHUNK, GROUP)
    packed = (n_groups, rows2, width)
    mids = pl.pallas_call(
        functools.partial(main_kernel, sizes),
        out_shape=(
            vm(packed, BF16),
            vm(packed, BF16),
            vm(packed, F32),
            vm(packed, F32),
            vm(per_head, BF16),
            vm(per_head, BF16),
            vm((n_groups, 8, 128), F32),
            vm(states, F32),
            vm(one_state, F32),
        ),
        in_specs=[anywhere] * 5,
        out_specs=(on_chip,) * 9,
        scratch_shapes=[
            vm((4,) + packed, BF16),
            vm((8, rows2, width), F32),
            vm(per_head, BF16),
            vm(per_head, BF16),
            vm(turned, BF16),
            vm(turned, BF16),
            vm(turned, BF16),
            vm(turned, BF16),
            vm((n_groups, GROUP, GROUP), F32),
            vm((n_heads, n_groups, GROUP, GROUP), BF16),
            vm((n_heads, GROUP, GROUP), BF16),
            vm(turned, F32),
            vm(turned, BF16),
            vm((2, rows2, width), F32),
            vm(states, F32),
            vm((n_heads, n_groups, width, width), BF16),
            pltpu.SMEM((2, n_seq), F32),
            pltpu.SMEM(doc_lengths.shape, jnp.int32),
            vm(slices, F32),
            vm(slices, F32),
            vm(one_state, F32),
            vm(slices, F32),
            vm(slices, F32),
            vm(sums, F32),
            vm((n_chunks, n_x * n_y, 2 * CHUNK, GROUP), F32),
            vm(sums, F32),
            vm(sums, F32),
            dma((4, n_groups // 2)),
        ]
        + [dma((n_heads,))] * 8
        + [dma((n_chunks,))] * 2
        + [dma],
        compiler_params=pltpu.CompilerParams(
            collective_id=0, has_side_effects=True, vmem_limit_bytes=44 << 20
        ),
        name="exchange_and_attend",
    )(doc_lengths, view(queries), view(keys), view(values), view(cotangent))
    mids = [pltpu.with_memory_space_constraint(m, pltpu.VMEM) for m in mids]
    results = pl.pallas_call(
        functools.partial(last_kernel, sizes),
        out_shape=(jax.ShapeDtypeStruct(packed, BF16),) * 4,
        in_specs=[on_chip] * 9,
        out_specs=(anywhere,) * 4,
        scratch_shapes=[
            vm((8, rows2, width), F32),
            vm((2,) + packed, BF16),
            dma((2, n_groups)),
            dma((2,)),
        ],
        compiler_params=pltpu.CompilerParams(vmem_limit_bytes=16 << 20),
        name="finish",
    )(*mids)
    return tuple(r.reshape(tokens_here, n_heads, width) for r in results)


def solution(mesh):
    n_x = 4
    spec = P("seq", "head", None)
    return jax.shard_map(
        functools.partial(per_device, (mesh.shape["seq"], n_x, mesh.shape["head"] // n_x)),
        mesh=mesh,
        in_specs=(spec,) * 4 + (P(),),
        out_specs=(spec,) * 4,
        check_vma=False,
    )
```

```python
import functools

import jax
import jax.numpy as jnp
from jax import lax
from jax.experimental import pallas as pl
from jax.experimental.pallas import tpu as pltpu
from jax.sharding import PartitionSpec as P

GROUP = 256
EPSILON = 1e-06
CHUNK = 4
MESH = pl.DeviceIdType.MESH
F32 = jnp.float32
BF16 = jnp.bfloat16
KK, VV = range(2)
QQ, GG = range(2)


def dot(a, b, ca=1, cb=0):
    return lax.dot_general(a, b, (((ca,), (cb,)), ((), ())), preferred_element_type=F32)


def flag(cond):
    return jnp.where(cond, 1.0, 0.0).astype(F32)


def doc_ends(doc_ref):
    ends, total = [], 0
    for j in range(doc_ref.shape[0]):
        total = total + doc_ref[j]
        ends.append(total)
    return ends


def seg_of(ends, p):
    s = (ends[0] <= p).astype(jnp.int32)
    for e in ends[1:]:
        s = s + (e <= p).astype(jnp.int32)
    return s


def last_end(ends, p):
    s = jnp.where(ends[0] <= p, ends[0], 0)
    for e in ends[1:]:
        s = jnp.where(e <= p, e, s)
    return s


def next_end(ends, p):
    s = ends[-1]
    for e in ends[-2::-1]:
        s = jnp.where(e > p, e, s)
    return s


def lane_gate(lower, limit):
    lane = lax.broadcasted_iota(jnp.int32, (16, GROUP), 1)
    one = jnp.where(lane >= limit if lower else lane < limit, 1.0, 0.0).astype(BF16)
    return jnp.concatenate([one] * 8, axis=0)


def far_first(n, per_chip):
    chips = n // per_chip

    def hops(d):
        c = d // per_chip
        return min(c, chips - c)

    return sorted(range(1, n), key=lambda d: -hops(d))


def main_kernel(
    sizes,
    doc_hbm,
    q_hbm,
    k_hbm,
    v_hbm,
    g_hbm,
    out_v,
    dq_v,
    dk_part,
    dv_part,
    k_after,
    v_after,
    weight,
    r_loc,
    r_in,
    raw,
    tmp,
    k_n,
    v_n,
    k_t,
    v_t,
    q_t,
    g_t,
    mask_ref,
    p_t,
    dp_t,
    o_t,
    dob_t,
    stage,
    s_loc,
    s_bf,
    q_before,
    q_lead,
    table,
    keep_ref,
    doc_ref,
    s_got,
    s_pre,
    s_in,
    r_got,
    r_pre,
    part,
    t_got,
    scale_a,
    scale_b,
    in_sem,
    s_send,
    s_recv,
    t_send,
    t_recv,
    r_send,
    r_recv,
    u_send,
    u_recv,
    a_send,
    a_recv,
    doc_sem,
):
    n_seq, n_x, n_y, n_groups, n_heads = sizes
    tokens = n_groups * GROUP
    n_head = n_x * n_y
    width_all = float(n_head * n_heads * 128)
    n_chunks = n_groups // CHUNK
    me = lax.axis_index("seq")
    head = lax.axis_index("head")
    mx = lax.rem(head, n_x)
    my = head // n_x
    slab = 128 // n_seq
    seq_order = far_first(n_seq, 2)
    head_order = sorted(
        range(1, n_head),
        key=lambda d: -(min(d % n_x, n_x - d % n_x) + min(d // n_x, n_y - d // n_x)),
    )

    def seq_peer(d):
        return lax.rem(me + d, n_seq)

    def head_peer(d, sign):
        x = lax.rem(mx + n_x + sign * (d % n_x), n_x)
        y = lax.rem(my + n_y + sign * (d // n_x), n_y)
        return y * n_x + x

    doc_copy = pltpu.make_async_copy(doc_hbm, doc_ref, doc_sem)
    doc_copy.start()
    sources = (k_hbm, v_hbm, q_hbm, g_hbm)

    pair = 2

    def load(a, g):
        two = pl.ds(g, pair)
        return pltpu.make_async_copy(sources[a].at[two], raw.at[a, two], in_sem.at[a, g // pair])

    @pl.loop(0, n_groups // pair)
    def _(i):
        load(0, i * pair).start()
        load(1, i * pair).start()

    @pl.loop(0, n_groups // pair)
    def _(i):
        load(2, i * pair).start()
        load(3, i * pair).start()

    barrier = pltpu.get_barrier_semaphore()
    for d in seq_order:
        pl.semaphore_signal(barrier, inc=1, device_id={"seq": seq_peer(d)}, device_id_type=MESH)
    for d in head_order:
        pl.semaphore_signal(barrier, inc=1, device_id={"head": head_peer(d, 1)}, device_id_type=MESH)

    doc_copy.wait()
    ends = doc_ends(doc_ref)
    shard_first = me * tokens
    after_s = seg_of(ends, shard_first + tokens)
    bs = seg_of(ends, shard_first - 1)

    def edges(g):
        first = shard_first + g * GROUP
        return (
            seg_of(ends, first - 1),
            seg_of(ends, first),
            seg_of(ends, first + GROUP - 1),
            seg_of(ends, first + GROUP),
        )

    def before_gate(g):
        first = shard_first + g * GROUP
        return lane_gate(False, next_end(ends, first - 1) - first)

    def tail_gate(g):
        first = shard_first + g * GROUP
        return lane_gate(True, last_end(ends, first + GROUP - 1) - first)

    def lead_gate(g):
        first = shard_first + g * GROUP
        return lane_gate(False, next_end(ends, first) - first)

    both_heads = range(n_heads)

    def spread(a, g, slot):
        tmp[slot] = raw[a, g].astype(F32)
        return [tmp[slot, pl.ds(h, GROUP, stride=n_heads), :].astype(BF16) for h in both_heads]

    def join(slot, parts):
        for h in both_heads:
            stage[slot, pl.ds(h, GROUP, stride=n_heads), :] = parts[h].astype(BF16).T.astype(F32)
        return stage[slot].astype(BF16)

    def put(ref, g, parts):
        for h in both_heads:
            ref[g, pl.ds(h, GROUP, stride=n_heads), :] = parts[h].astype(F32).T

    def key_states(groups, h):
        added = [dot(v_t[h, g] * tail_gate(g), k_n[h, g]) for g in groups]
        for g, new in zip(groups, added):
            bc, c0, c1, ac = edges(g)
            s_loc[h, g + 1] = flag(c1 == bc) * s_loc[h, g] + new

    def hand(src, dst, send, recv, d):
        return pltpu.make_async_remote_copy(
            src_ref=src,
            dst_ref=dst,
            send_sem=send,
            recv_sem=recv,
            device_id={"seq": seq_peer(d)},
            device_id_type=MESH,
        )

    def everything(got, h, send, recv):
        return hand(got.at[h, pl.ds(0, n_seq - 1)], got.at[h, pl.ds(0, n_seq - 1)], send, recv, 1)

    def rows(ref, h, i):
        return ref.at[h, pl.ds(pl.multiple_of(i * slab, slab), slab)]

    class Run:
        def __init__(self, ref, slot):
            self.ref, self.slot = ref, slot

        @property
        def at(self):
            return self

        def __getitem__(self, index):
            h, rest = index
            return self.ref.at[h, self.slot, rest]

    s_run, r_run = Run(s_loc, n_groups), Run(r_loc, 0)

    def scatter(h, run, got, send, recv):
        for d in seq_order:
            hand(rows(run, h, seq_peer(d)), got.at[h, me], send.at[h], recv.at[h], d).start()

    def combine(h, run, got, pre, into, send, recv, backward):
        mine = pl.ds(pl.multiple_of(me * slab, slab), slab)
        got[h, me] = run.ref[h, run.slot, mine, :]
        everything(got, h, send.at[h], recv.at[h]).wait_recv()
        carry = jnp.zeros((slab, 128), F32)
        for i in range(n_seq - 1, -1, -1) if backward else range(n_seq):
            pre[h, i] = carry
            carry = keep_ref[1 if backward else 0, i] * carry + got[h, i]
        into[h, mine, :] = pre[h, me]

    def give(h, pre, into, send, recv):
        for d in seq_order:
            hand(pre.at[h, seq_peer(d)], rows(into, h, me), send.at[h], recv.at[h], d).start()

    def give_done(h, got, send, recv):
        everything(got, h, send.at[h], recv.at[h]).wait_recv()

    def sends_done(h, got, *pairs):
        for send, recv in pairs:
            everything(got, h, send.at[h], recv.at[h]).wait_send()

    for h in both_heads:
        s_loc[h, 0] = jnp.zeros((128, 128), F32)

    def batch(i):
        return [i * CHUNK + u for u in range(CHUNK)]

    def take_keys_values(groups):
        for half in range(CHUNK // pair):
            load(0, groups[half * pair]).wait()
            load(1, groups[half * pair]).wait()
        for u, g in enumerate(groups):
            for h, x in enumerate(spread(1, g, 2 * u + 1)):
                v_n[h, g] = x
                v_t[h, g] = x.T
            for h, x in enumerate(spread(0, g, 2 * u)):
                k_n[h, g] = x

    @pl.loop(0, n_groups // CHUNK)
    def _(i):
        take_keys_values(batch(i))
        key_states(batch(i), 0)

    pl.semaphore_wait(barrier, n_seq - 1 + n_head - 1)
    scatter(0, s_run, s_got, s_send, s_recv)

    for h in range(1, n_heads):

        @pl.loop(0, n_groups // CHUNK)
        def _(i):
            key_states(batch(i), h)

        scatter(h, s_run, s_got, s_send, s_recv)

    for i in range(n_seq):
        first = i * tokens
        keep_ref[0, i] = flag(seg_of(ends, first + tokens - 1) == seg_of(ends, first - 1))
        keep_ref[1, i] = flag(seg_of(ends, first) == seg_of(ends, first + tokens))

    def build_mask(g):
        first = shard_first + g * GROUP
        lane8 = lax.broadcasted_iota(jnp.int32, (8, GROUP), 1)
        start = jnp.broadcast_to((last_end(ends, lane8 + first) - first)[0:1], (GROUP, GROUP))
        key = lax.broadcasted_iota(jnp.int32, (GROUP, GROUP), 0)
        query = lax.broadcasted_iota(jnp.int32, (GROUP, GROUP), 1)
        mask_ref[g] = jnp.where(jnp.logical_and(key >= start, key <= query), 1.0, 0.0).astype(F32)

    def intra(i):
        groups = [i * pair + u for u in range(pair)]
        load(2, groups[0]).wait()
        for u, g in enumerate(groups):
            build_mask(g)
            for h, x in enumerate(spread(2, g, u)):
                q_t[h, g] = x.T
                k_t[h, g] = k_n[h, g].T
        for g in groups:
            for h in both_heads:
                p_t[h, g] = (dot(k_n[h, g], q_t[h, g]) * mask_ref[g]).astype(BF16)
        for g in groups:
            for h in both_heads:
                o_t[h, g] = dot(v_t[h, g], p_t[h, g])

    n_pairs = n_groups // pair

    def take_cotangent(groups):
        for half in range(CHUNK // pair):
            load(3, groups[half * pair]).wait()
        for u, g in enumerate(groups):
            for h, x in enumerate(spread(3, g, u)):
                g_t[h, g] = x.T

    early = (2 * n_pairs) // 3

    @pl.loop(0, early)
    def _(i):
        intra(i)

    combine(0, s_run, s_got, s_pre, s_in, s_send, s_recv, False)
    give(0, s_pre, s_in, t_send, t_recv)
    intra(early)
    for h in range(1, n_heads):
        combine(h, s_run, s_got, s_pre, s_in, s_send, s_recv, False)
        give(h, s_pre, s_in, t_send, t_recv)
    for i in range(early + 1, n_pairs):
        intra(i)

    @pl.loop(0, n_groups // CHUNK)
    def _(i):
        take_cotangent(batch(i))

    @pl.loop(0, n_groups)
    def _(g):
        bc, c0, c1, ac = edges(g)
        table[0, g] = flag(bc == bs)
        table[1, g] = flag(c0 == ac)
        before, lead = before_gate(g), lead_gate(g)
        for h in both_heads:
            q_before[h, g] = q_t[h, g] * before
            q_lead[h, g] = q_t[h, g] * lead

    def outer(groups, h):
        for g in groups:
            s_bf[h, g] = (s_loc[h, g] + table[0, g] * s_in[h]).astype(BF16)
        more = [dot(s_bf[h, g], q_before[h, g]) for g in groups]
        for g, x in zip(groups, more):
            o = o_t[h, g] + x
            o_t[h, g] = o
            c, r = g // CHUNK, lax.rem(g, CHUNK)
            squares = jnp.sum(o * o, axis=0, keepdims=True)
            inner = jnp.sum(g_t[h, g].astype(F32) * o, axis=0, keepdims=True)
            one, two = pl.ds(r, 1), pl.ds(CHUNK + r, 1)
            if h == 0:
                part[c, one, :] = squares
                part[c, two, :] = inner
            else:
                part[c, one, :] += squares
                part[c, two, :] += inner

    for h in range(n_heads - 1):
        give_done(h, s_pre, t_send, t_recv)

        @pl.loop(0, n_groups // CHUNK)
        def _(i):
            outer([i * CHUNK + u for u in range(CHUNK)], h)

    give_done(n_heads - 1, s_pre, t_send, t_recv)

    def part_copy(c, d):
        return pltpu.make_async_remote_copy(
            src_ref=part.at[c],
            dst_ref=t_got.at[c, head],
            send_sem=a_send.at[c],
            recv_sem=a_recv.at[c],
            device_id={"head": head_peer(d, 1)},
            device_id_type=MESH,
        )

    def all_parts(c):
        return pltpu.make_async_remote_copy(
            src_ref=t_got.at[c, pl.ds(0, n_head - 1)],
            dst_ref=t_got.at[c, pl.ds(0, n_head - 1)],
            send_sem=a_send.at[c],
            recv_sem=a_recv.at[c],
            device_id={"head": head_peer(1, 1)},
            device_id_type=MESH,
        )

    for c in range(n_chunks - 1, -1, -1):

        outer([c * CHUNK + u for u in range(CHUNK)], n_heads - 1)

        for d in head_order:
            part_copy(c, d).start()
        t_got[c, head] = part[c]

    for h in both_heads:
        r_loc[h, n_groups] = jnp.zeros((128, 128), F32)

    def wide(ref, g):
        c, r = g // CHUNK, lax.rem(g, CHUNK)
        return jnp.broadcast_to(ref[c, pl.ds(r, 1), :], (128, GROUP))

    def back_states(groups, heads):
        for g in groups:
            for h in heads:
                dob_t[h, g] = (g_t[h, g].astype(F32) * wide(scale_a, g) - o_t[h, g] * wide(scale_b, g)).astype(BF16)
        added = [[dot(q_lead[h, g], dob_t[h, g], 1, 1) for h in heads] for g in groups]
        for g, row in zip(groups, added):
            for h, new in zip(heads, row):
                r_loc[h, g] = table[1, g] * r_loc[h, g + 1] + new

    def gather_part(c):
        all_parts(c).wait_recv()
        value = t_got[c, 0]
        for i in range(1, n_head):
            value = value + t_got[c, i]
        a = 1.0 / jnp.sqrt(value[:CHUNK] / width_all + EPSILON)
        scale_a[c, 0:CHUNK] = a
        scale_b[c, 0:CHUNK] = a * a * (a * value[CHUNK:] / width_all)

    for c in range(n_chunks - 1, 0, -1):
        gather_part(c)

        back_states([c * CHUNK + CHUNK - 1 - u for u in range(CHUNK)], both_heads)

    gather_part(0)
    for h in both_heads:

        back_states([CHUNK - 1 - u for u in range(CHUNK)], [h])

        scatter(h, r_run, r_got, r_send, r_recv)

    def inner_back(g):
        before = before_gate(g)
        bc, c0, c1, ac = edges(g)
        weight[g] = jnp.broadcast_to(flag(ac == after_s), (8, 128))
        first = shard_first + g * GROUP
        row = lax.broadcasted_iota(jnp.int32, (GROUP, 128), 0)
        after = jnp.where(row >= last_end(ends, first + GROUP) - first, 1.0, 0.0).astype(BF16)
        for h in both_heads:
            dp_t[h] = (dot(v_n[h, g], dob_t[h, g]) * mask_ref[g]).astype(BF16)
        put(dv_part, g, [dot(dob_t[h, g], p_t[h, g], 1, 1) for h in both_heads])
        out_v[g] = join(0, [o_t[h, g] * wide(scale_a, g) for h in both_heads])
        more = [dot(s_bf[h, g], dob_t[h, g] * before, 0, 0) for h in both_heads]
        dq_v[g] = join(1, [dot(k_t[h, g], dp_t[h]) + more[h] for h in both_heads])
        put(dk_part, g, [dot(q_t[h, g], dp_t[h], 1, 1) for h in both_heads])
        for h in both_heads:
            k_after[h, g] = k_n[h, g] * after
            v_after[h, g] = v_n[h, g] * after

    cut1 = n_groups // 2

    @pl.loop(0, cut1)
    def _(g):
        inner_back(g)

    combine(0, r_run, r_got, r_pre, r_in, r_send, r_recv, True)
    give(0, r_pre, r_in, u_send, u_recv)

    for h in range(1, n_heads):
        combine(h, r_run, r_got, r_pre, r_in, r_send, r_recv, True)
        give(h, r_pre, r_in, u_send, u_recv)

    @pl.loop(cut1, n_groups)
    def _(g):
        inner_back(g)

    for h in both_heads:
        sends_done(h, s_pre, (s_send, s_recv), (t_send, t_recv), (r_send, r_recv))
    for c in range(n_chunks):
        all_parts(c).wait_send()
    for h in both_heads:
        give_done(h, r_pre, u_send, u_recv)
        sends_done(h, r_pre, (u_send, u_recv))


def last_kernel(
    sizes,
    out_v,
    dq_v,
    dk_part,
    dv_part,
    k_after,
    v_after,
    weight,
    r_loc,
    r_in,
    out_hbm,
    dq_hbm,
    dk_hbm,
    dv_hbm,
    stage,
    done,
    sem,
    whole,
):
    n_seq, n_x, n_y, n_groups, n_heads = sizes
    copies = [
        pltpu.make_async_copy(out_v, out_hbm, whole.at[0]),
        pltpu.make_async_copy(dq_v, dq_hbm, whole.at[1]),
    ]
    for c in copies:
        c.start()
    targets = (dk_hbm, dv_hbm)
    parts = (dk_part, dv_part)
    batch = 12

    def store(i, g):
        return pltpu.make_async_copy(done.at[i, g], targets[i].at[g], sem.at[i, g])

    for step in range(n_groups // batch):
        for u in range(batch):
            g = step * batch + u
            w = jnp.broadcast_to(weight[g, 0:1, :], (128, 128))
            for h in range(n_heads):
                state = (r_loc[h, g + 1] + w * r_in[h]).astype(BF16)
                even = pl.ds(h, GROUP, stride=n_heads)
                stage[2 * u, even, :] = dot(v_after[h, g], state, 1, 1)
                stage[2 * u + 1, even, :] = dot(k_after[h, g], state)
            for i in range(2):
                done[i, g] = (stage[2 * u + i] + parts[i][g]).astype(BF16)
                store(i, g).start()

    @pl.loop(0, n_groups)
    def _(g):
        for i in range(2):
            store(i, g).wait()

    for c in copies:
        c.wait()


def per_device(sizes, queries, keys, values, cotangent, doc_lengths):
    tokens_here, n_heads, width = queries.shape
    n_seq, n_x, n_y = sizes
    n_groups = tokens_here // GROUP
    n_chunks = n_groups // CHUNK
    rows2 = GROUP * n_heads
    slab = width // n_seq
    sizes = (n_seq, n_x, n_y, n_groups, n_heads)
    view = lambda x: x.reshape(n_groups, rows2, width)
    dma = pltpu.SemaphoreType.DMA
    vm = pltpu.VMEM
    anywhere = pl.BlockSpec(memory_space=pl.ANY)
    on_chip = pl.BlockSpec(memory_space=pltpu.VMEM)
    per_head = (n_heads, n_groups, GROUP, width)
    turned = (n_heads, n_groups, width, GROUP)
    states = (n_heads, n_groups + 1, width, width)
    one_state = (n_heads, width, width)
    slices = (n_heads, n_seq, slab, width)
    sums = (n_chunks, 2 * CHUNK, GROUP)
    packed = (n_groups, rows2, width)
    mids = pl.pallas_call(
        functools.partial(main_kernel, sizes),
        out_shape=(
            vm(packed, BF16),
            vm(packed, BF16),
            vm(packed, F32),
            vm(packed, F32),
            vm(per_head, BF16),
            vm(per_head, BF16),
            vm((n_groups, 8, 128), F32),
            vm(states, F32),
            vm(one_state, F32),
        ),
        in_specs=[anywhere] * 5,
        out_specs=(on_chip,) * 9,
        scratch_shapes=[
            vm((4,) + packed, BF16),
            vm((8, rows2, width), F32),
            vm(per_head, BF16),
            vm(per_head, BF16),
            vm(turned, BF16),
            vm(turned, BF16),
            vm(turned, BF16),
            vm(turned, BF16),
            vm((n_groups, GROUP, GROUP), F32),
            vm((n_heads, n_groups, GROUP, GROUP), BF16),
            vm((n_heads, GROUP, GROUP), BF16),
            vm(turned, F32),
            vm(turned, BF16),
            vm((2, rows2, width), F32),
            vm(states, F32),
            vm((n_heads, n_groups, width, width), BF16),
            vm(turned, BF16),
            vm(turned, BF16),
            pltpu.SMEM((2, n_groups), F32),
            pltpu.SMEM((2, n_seq), F32),
            pltpu.SMEM(doc_lengths.shape, jnp.int32),
            vm(slices, F32),
            vm(slices, F32),
            vm(one_state, F32),
            vm(slices, F32),
            vm(slices, F32),
            vm(sums, F32),
            vm((n_chunks, n_x * n_y, 2 * CHUNK, GROUP), F32),
            vm(sums, F32),
            vm(sums, F32),
            dma((4, n_groups // 2)),
        ]
        + [dma((n_heads,))] * 8
        + [dma((n_chunks,))] * 2
        + [dma],
        compiler_params=pltpu.CompilerParams(
            collective_id=0, has_side_effects=True, vmem_limit_bytes=44 << 20
        ),
        name="exchange_and_attend",
    )(doc_lengths, view(queries), view(keys), view(values), view(cotangent))
    mids = [pltpu.with_memory_space_constraint(m, pltpu.VMEM) for m in mids]
    results = pl.pallas_call(
        functools.partial(last_kernel, sizes),
        out_shape=(jax.ShapeDtypeStruct(packed, BF16),) * 4,
        in_specs=[on_chip] * 9,
        out_specs=(anywhere,) * 4,
        scratch_shapes=[
            vm((24, rows2, width), F32),
            vm((2,) + packed, BF16),
            dma((2, n_groups)),
            dma((2,)),
        ],
        compiler_params=pltpu.CompilerParams(vmem_limit_bytes=16 << 20),
        name="finish",
    )(*mids)
    return tuple(r.reshape(tokens_here, n_heads, width) for r in results)


def solution(mesh):
    n_x = 4
    spec = P("seq", "head", None)
    return jax.shard_map(
        functools.partial(per_device, (mesh.shape["seq"], n_x, mesh.shape["head"] // n_x)),
        mesh=mesh,
        in_specs=(spec,) * 4 + (P(),),
        out_specs=(spec,) * 4,
        check_vma=False,
    )
```

```python
import functools

import jax
import jax.numpy as jnp
from jax import lax
from jax.experimental import pallas as pl
from jax.experimental.pallas import tpu as pltpu
from jax.sharding import PartitionSpec as P

GROUP = 256
EPSILON = 1e-06
CHUNK = 4
MESH = pl.DeviceIdType.MESH
F32 = jnp.float32
BF16 = jnp.bfloat16
KK, VV = range(2)
QQ, GG = range(2)


def dot(a, b, ca=1, cb=0):
    return lax.dot_general(a, b, (((ca,), (cb,)), ((), ())), preferred_element_type=F32)


def flag(cond):
    return jnp.where(cond, 1.0, 0.0).astype(F32)


def doc_ends(doc_ref):
    ends, total = [], 0
    for j in range(doc_ref.shape[0]):
        total = total + doc_ref[j]
        ends.append(total)
    return ends


def seg_of(ends, p):
    s = (ends[0] <= p).astype(jnp.int32)
    for e in ends[1:]:
        s = s + (e <= p).astype(jnp.int32)
    return s


def last_end(ends, p):
    s = jnp.where(ends[0] <= p, ends[0], 0)
    for e in ends[1:]:
        s = jnp.where(e <= p, e, s)
    return s


def next_end(ends, p):
    s = ends[-1]
    for e in ends[-2::-1]:
        s = jnp.where(e > p, e, s)
    return s


def lane_gate(lower, limit):
    lane = lax.broadcasted_iota(jnp.int32, (16, GROUP), 1)
    one = jnp.where(lane >= limit if lower else lane < limit, 1.0, 0.0).astype(BF16)
    return jnp.concatenate([one] * 8, axis=0)


def far_first(n, per_chip):
    chips = n // per_chip

    def hops(d):
        c = d // per_chip
        return min(c, chips - c)

    return sorted(range(1, n), key=lambda d: -hops(d))


def main_kernel(
    sizes,
    doc_hbm,
    q_hbm,
    k_hbm,
    v_hbm,
    g_hbm,
    out_v,
    dq_v,
    dk_part,
    dv_part,
    k_after,
    v_after,
    weight,
    r_loc,
    r_in,
    raw,
    tmp,
    k_n,
    v_n,
    k_t,
    v_t,
    q_t,
    g_t,
    mask_ref,
    p_t,
    dp_t,
    o_t,
    dob_t,
    stage,
    s_loc,
    s_bf,
    q_before,
    q_lead,
    table,
    keep_ref,
    doc_ref,
    s_got,
    s_pre,
    s_in,
    r_got,
    r_pre,
    part,
    t_got,
    scale_a,
    scale_b,
    in_sem,
    s_send,
    s_recv,
    t_send,
    t_recv,
    r_send,
    r_recv,
    u_send,
    u_recv,
    a_send,
    a_recv,
    doc_sem,
):
    n_seq, n_x, n_y, n_groups, n_heads = sizes
    tokens = n_groups * GROUP
    n_head = n_x * n_y
    width_all = float(n_head * n_heads * 128)
    n_chunks = n_groups // CHUNK
    me = lax.axis_index("seq")
    head = lax.axis_index("head")
    mx = lax.rem(head, n_x)
    my = head // n_x
    slab = 128 // n_seq
    seq_order = far_first(n_seq, 2)
    head_order = sorted(
        range(1, n_head),
        key=lambda d: -(min(d % n_x, n_x - d % n_x) + min(d // n_x, n_y - d // n_x)),
    )

    def seq_peer(d):
        return lax.rem(me + d, n_seq)

    def head_peer(d, sign):
        x = lax.rem(mx + n_x + sign * (d % n_x), n_x)
        y = lax.rem(my + n_y + sign * (d // n_x), n_y)
        return y * n_x + x

    doc_copy = pltpu.make_async_copy(doc_hbm, doc_ref, doc_sem)
    doc_copy.start()
    sources = (k_hbm, v_hbm, q_hbm, g_hbm)

    pair = 2

    def load(a, g):
        two = pl.ds(g, pair)
        return pltpu.make_async_copy(sources[a].at[two], raw.at[a, two], in_sem.at[a, g // pair])

    @pl.loop(0, n_groups // pair)
    def _(i):
        load(0, i * pair).start()
        load(1, i * pair).start()

    @pl.loop(0, n_groups // pair)
    def _(i):
        load(2, i * pair).start()
        load(3, i * pair).start()

    barrier = pltpu.get_barrier_semaphore()
    for d in seq_order:
        pl.semaphore_signal(barrier, inc=1, device_id={"seq": seq_peer(d)}, device_id_type=MESH)
    for d in head_order:
        pl.semaphore_signal(barrier, inc=1, device_id={"head": head_peer(d, 1)}, device_id_type=MESH)

    doc_copy.wait()
    ends = doc_ends(doc_ref)
    shard_first = me * tokens
    after_s = seg_of(ends, shard_first + tokens)
    bs = seg_of(ends, shard_first - 1)

    def edges(g):
        first = shard_first + g * GROUP
        return (
            seg_of(ends, first - 1),
            seg_of(ends, first),
            seg_of(ends, first + GROUP - 1),
            seg_of(ends, first + GROUP),
        )

    def before_gate(g):
        first = shard_first + g * GROUP
        return lane_gate(False, next_end(ends, first - 1) - first)

    def tail_gate(g):
        first = shard_first + g * GROUP
        return lane_gate(True, last_end(ends, first + GROUP - 1) - first)

    def lead_gate(g):
        first = shard_first + g * GROUP
        return lane_gate(False, next_end(ends, first) - first)

    both_heads = range(n_heads)

    def spread(a, g, slot):
        tmp[slot] = raw[a, g].astype(F32)
        return [tmp[slot, pl.ds(h, GROUP, stride=n_heads), :].astype(BF16) for h in both_heads]

    def join(slot, parts):
        for h in both_heads:
            stage[slot, pl.ds(h, GROUP, stride=n_heads), :] = parts[h].astype(BF16).T.astype(F32)
        return stage[slot].astype(BF16)

    def put(ref, g, parts):
        for h in both_heads:
            ref[g, pl.ds(h, GROUP, stride=n_heads), :] = parts[h].astype(F32).T

    def key_states(groups, h):
        added = [dot(v_t[h, g] * tail_gate(g), k_n[h, g]) for g in groups]
        for g, new in zip(groups, added):
            bc, c0, c1, ac = edges(g)
            s_loc[h, g + 1] = flag(c1 == bc) * s_loc[h, g] + new

    def hand(src, dst, send, recv, d):
        return pltpu.make_async_remote_copy(
            src_ref=src,
            dst_ref=dst,
            send_sem=send,
            recv_sem=recv,
            device_id={"seq": seq_peer(d)},
            device_id_type=MESH,
        )

    def everything(got, h, send, recv):
        return hand(got.at[h, pl.ds(0, n_seq - 1)], got.at[h, pl.ds(0, n_seq - 1)], send, recv, 1)

    def rows(ref, h, i):
        return ref.at[h, pl.ds(pl.multiple_of(i * slab, slab), slab)]

    class Run:
        def __init__(self, ref, slot):
            self.ref, self.slot = ref, slot

        @property
        def at(self):
            return self

        def __getitem__(self, index):
            h, rest = index
            return self.ref.at[h, self.slot, rest]

    s_run, r_run = Run(s_loc, n_groups), Run(r_loc, 0)

    def scatter(h, run, got, send, recv):
        for d in seq_order:
            hand(rows(run, h, seq_peer(d)), got.at[h, me], send.at[h], recv.at[h], d).start()

    def combine(h, run, got, pre, into, send, recv, backward):
        mine = pl.ds(pl.multiple_of(me * slab, slab), slab)
        got[h, me] = run.ref[h, run.slot, mine, :]
        everything(got, h, send.at[h], recv.at[h]).wait_recv()
        carry = jnp.zeros((slab, 128), F32)
        for i in range(n_seq - 1, -1, -1) if backward else range(n_seq):
            pre[h, i] = carry
            carry = keep_ref[1 if backward else 0, i] * carry + got[h, i]
        into[h, mine, :] = pre[h, me]

    def give(h, pre, into, send, recv):
        for d in seq_order:
            hand(pre.at[h, seq_peer(d)], rows(into, h, me), send.at[h], recv.at[h], d).start()

    def give_done(h, got, send, recv):
        everything(got, h, send.at[h], recv.at[h]).wait_recv()

    def sends_done(h, got, *pairs):
        for send, recv in pairs:
            everything(got, h, send.at[h], recv.at[h]).wait_send()

    for h in both_heads:
        s_loc[h, 0] = jnp.zeros((128, 128), F32)

    def batch(i):
        return [i * CHUNK + u for u in range(CHUNK)]

    def take_keys_values(groups):
        for half in range(CHUNK // pair):
            load(0, groups[half * pair]).wait()
            load(1, groups[half * pair]).wait()
        for u, g in enumerate(groups):
            for h, x in enumerate(spread(1, g, 2 * u + 1)):
                v_n[h, g] = x
                v_t[h, g] = x.T
            for h, x in enumerate(spread(0, g, 2 * u)):
                k_n[h, g] = x

    @pl.loop(0, n_groups // CHUNK)
    def _(i):
        take_keys_values(batch(i))
        for h in both_heads:
            key_states(batch(i), h)

    pl.semaphore_wait(barrier, n_seq - 1 + n_head - 1)
    for h in both_heads:
        scatter(h, s_run, s_got, s_send, s_recv)

    for i in range(n_seq):
        first = i * tokens
        keep_ref[0, i] = flag(seg_of(ends, first + tokens - 1) == seg_of(ends, first - 1))
        keep_ref[1, i] = flag(seg_of(ends, first) == seg_of(ends, first + tokens))

    def build_mask(g):
        first = shard_first + g * GROUP
        lane8 = lax.broadcasted_iota(jnp.int32, (8, GROUP), 1)
        start = jnp.broadcast_to((last_end(ends, lane8 + first) - first)[0:1], (GROUP, GROUP))
        key = lax.broadcasted_iota(jnp.int32, (GROUP, GROUP), 0)
        query = lax.broadcasted_iota(jnp.int32, (GROUP, GROUP), 1)
        mask_ref[g] = jnp.where(jnp.logical_and(key >= start, key <= query), 1.0, 0.0).astype(F32)

    def intra(i):
        groups = [i * pair + u for u in range(pair)]
        load(2, groups[0]).wait()
        for u, g in enumerate(groups):
            build_mask(g)
            for h, x in enumerate(spread(2, g, u)):
                q_t[h, g] = x.T
                k_t[h, g] = k_n[h, g].T
        for g in groups:
            for h in both_heads:
                p_t[h, g] = (dot(k_n[h, g], q_t[h, g]) * mask_ref[g]).astype(BF16)
        for g in groups:
            for h in both_heads:
                o_t[h, g] = dot(v_t[h, g], p_t[h, g])

    n_pairs = n_groups // pair

    def take_cotangent(groups):
        for half in range(CHUNK // pair):
            load(3, groups[half * pair]).wait()
        for u, g in enumerate(groups):
            for h, x in enumerate(spread(3, g, u)):
                g_t[h, g] = x.T

    early = (2 * n_pairs) // 3

    @pl.loop(0, n_pairs)
    def _(i):
        intra(i)

        @pl.when(i == early - 1)
        def _():
            for h in both_heads:
                combine(h, s_run, s_got, s_pre, s_in, s_send, s_recv, False)
                give(h, s_pre, s_in, t_send, t_recv)

    @pl.loop(0, n_groups // CHUNK)
    def _(i):
        take_cotangent(batch(i))

    @pl.loop(0, n_groups)
    def _(g):
        bc, c0, c1, ac = edges(g)
        table[0, g] = flag(bc == bs)
        table[1, g] = flag(c0 == ac)
        before, lead = before_gate(g), lead_gate(g)
        for h in both_heads:
            q_before[h, g] = q_t[h, g] * before
            q_lead[h, g] = q_t[h, g] * lead

    def outer(groups, h):
        for g in groups:
            s_bf[h, g] = (s_loc[h, g] + table[0, g] * s_in[h]).astype(BF16)
        more = [dot(s_bf[h, g], q_before[h, g]) for g in groups]
        for g, x in zip(groups, more):
            o = o_t[h, g] + x
            o_t[h, g] = o
            c, r = g // CHUNK, lax.rem(g, CHUNK)
            squares = jnp.sum(o * o, axis=0, keepdims=True)
            inner = jnp.sum(g_t[h, g].astype(F32) * o, axis=0, keepdims=True)
            one, two = pl.ds(r, 1), pl.ds(CHUNK + r, 1)
            if h == 0:
                part[c, one, :] = squares
                part[c, two, :] = inner
            else:
                part[c, one, :] += squares
                part[c, two, :] += inner

    for h in range(n_heads - 1):
        give_done(h, s_pre, t_send, t_recv)

        @pl.loop(0, n_groups // CHUNK)
        def _(i):
            outer([i * CHUNK + u for u in range(CHUNK)], h)

    give_done(n_heads - 1, s_pre, t_send, t_recv)

    def part_copy(c, d):
        return pltpu.make_async_remote_copy(
            src_ref=part.at[c],
            dst_ref=t_got.at[c, head],
            send_sem=a_send.at[c],
            recv_sem=a_recv.at[c],
            device_id={"head": head_peer(d, 1)},
            device_id_type=MESH,
        )

    def all_parts(c):
        return pltpu.make_async_remote_copy(
            src_ref=t_got.at[c, pl.ds(0, n_head - 1)],
            dst_ref=t_got.at[c, pl.ds(0, n_head - 1)],
            send_sem=a_send.at[c],
            recv_sem=a_recv.at[c],
            device_id={"head": head_peer(1, 1)},
            device_id_type=MESH,
        )

    @pl.loop(0, n_chunks)
    def _(i):
        c = n_chunks - 1 - i
        outer(batch(c), n_heads - 1)
        for d in head_order:
            part_copy(c, d).start()
        t_got[c, head] = part[c]

    for h in both_heads:
        r_loc[h, n_groups] = jnp.zeros((128, 128), F32)

    def wide(ref, g):
        c, r = g // CHUNK, lax.rem(g, CHUNK)
        return jnp.broadcast_to(ref[c, pl.ds(r, 1), :], (128, GROUP))

    def back_states(groups, heads):
        for g in groups:
            for h in heads:
                dob_t[h, g] = (g_t[h, g].astype(F32) * wide(scale_a, g) - o_t[h, g] * wide(scale_b, g)).astype(BF16)
        added = [[dot(q_lead[h, g], dob_t[h, g], 1, 1) for h in heads] for g in groups]
        for g, row in zip(groups, added):
            for h, new in zip(heads, row):
                r_loc[h, g] = table[1, g] * r_loc[h, g + 1] + new

    def gather_part(c):
        all_parts(c).wait_recv()
        value = t_got[c, 0]
        for i in range(1, n_head):
            value = value + t_got[c, i]
        a = 1.0 / jnp.sqrt(value[:CHUNK] / width_all + EPSILON)
        scale_a[c, 0:CHUNK] = a
        scale_b[c, 0:CHUNK] = a * a * (a * value[CHUNK:] / width_all)

    @pl.loop(0, n_chunks)
    def _(i):
        c = n_chunks - 1 - i
        gather_part(c)
        back_states(batch(c)[::-1], both_heads)

    for h in both_heads:
        scatter(h, r_run, r_got, r_send, r_recv)

    def inner_back(g):
        before = before_gate(g)
        bc, c0, c1, ac = edges(g)
        weight[g] = jnp.broadcast_to(flag(ac == after_s), (8, 128))
        first = shard_first + g * GROUP
        row = lax.broadcasted_iota(jnp.int32, (GROUP, 128), 0)
        after = jnp.where(row >= last_end(ends, first + GROUP) - first, 1.0, 0.0).astype(BF16)
        for h in both_heads:
            dp_t[h] = (dot(v_n[h, g], dob_t[h, g]) * mask_ref[g]).astype(BF16)
        put(dv_part, g, [dot(dob_t[h, g], p_t[h, g], 1, 1) for h in both_heads])
        out_v[g] = join(0, [o_t[h, g] * wide(scale_a, g) for h in both_heads])
        more = [dot(s_bf[h, g], dob_t[h, g] * before, 0, 0) for h in both_heads]
        dq_v[g] = join(1, [dot(k_t[h, g], dp_t[h]) + more[h] for h in both_heads])
        put(dk_part, g, [dot(q_t[h, g], dp_t[h], 1, 1) for h in both_heads])
        for h in both_heads:
            k_after[h, g] = k_n[h, g] * after
            v_after[h, g] = v_n[h, g] * after

    @pl.loop(0, n_groups)
    def _(g):
        inner_back(g)

        @pl.when(g == n_groups // 2 - 1)
        def _():
            for h in both_heads:
                combine(h, r_run, r_got, r_pre, r_in, r_send, r_recv, True)
                give(h, r_pre, r_in, u_send, u_recv)

    for h in both_heads:
        sends_done(h, s_pre, (s_send, s_recv), (t_send, t_recv), (r_send, r_recv))
    for c in range(n_chunks):
        all_parts(c).wait_send()
    for h in both_heads:
        give_done(h, r_pre, u_send, u_recv)
        sends_done(h, r_pre, (u_send, u_recv))


def last_kernel(
    sizes,
    out_v,
    dq_v,
    dk_part,
    dv_part,
    k_after,
    v_after,
    weight,
    r_loc,
    r_in,
    out_hbm,
    dq_hbm,
    dk_hbm,
    dv_hbm,
    stage,
    done,
    sem,
    whole,
):
    n_seq, n_x, n_y, n_groups, n_heads = sizes
    copies = [
        pltpu.make_async_copy(out_v, out_hbm, whole.at[0]),
        pltpu.make_async_copy(dq_v, dq_hbm, whole.at[1]),
    ]
    for c in copies:
        c.start()
    targets = (dk_hbm, dv_hbm)
    parts = (dk_part, dv_part)
    batch = 4

    def store(i, g):
        return pltpu.make_async_copy(done.at[i, g], targets[i].at[g], sem.at[i, g])

    @pl.loop(0, n_groups // batch)
    def _(step):
        for u in range(batch):
            g = step * batch + u
            w = jnp.broadcast_to(weight[g, 0:1, :], (128, 128))
            for h in range(n_heads):
                state = (r_loc[h, g + 1] + w * r_in[h]).astype(BF16)
                even = pl.ds(h, GROUP, stride=n_heads)
                stage[2 * u, even, :] = dot(v_after[h, g], state, 1, 1)
                stage[2 * u + 1, even, :] = dot(k_after[h, g], state)
            for i in range(2):
                done[i, g] = (stage[2 * u + i] + parts[i][g]).astype(BF16)
                store(i, g).start()

    @pl.loop(0, n_groups)
    def _(g):
        for i in range(2):
            store(i, g).wait()

    for c in copies:
        c.wait()


def per_device(sizes, queries, keys, values, cotangent, doc_lengths):
    tokens_here, n_heads, width = queries.shape
    n_seq, n_x, n_y = sizes
    n_groups = tokens_here // GROUP
    n_chunks = n_groups // CHUNK
    rows2 = GROUP * n_heads
    slab = width // n_seq
    sizes = (n_seq, n_x, n_y, n_groups, n_heads)
    view = lambda x: x.reshape(n_groups, rows2, width)
    dma = pltpu.SemaphoreType.DMA
    vm = pltpu.VMEM
    anywhere = pl.BlockSpec(memory_space=pl.ANY)
    on_chip = pl.BlockSpec(memory_space=pltpu.VMEM)
    per_head = (n_heads, n_groups, GROUP, width)
    turned = (n_heads, n_groups, width, GROUP)
    states = (n_heads, n_groups + 1, width, width)
    one_state = (n_heads, width, width)
    slices = (n_heads, n_seq, slab, width)
    sums = (n_chunks, 2 * CHUNK, GROUP)
    packed = (n_groups, rows2, width)
    mids = pl.pallas_call(
        functools.partial(main_kernel, sizes),
        out_shape=(
            vm(packed, BF16),
            vm(packed, BF16),
            vm(packed, F32),
            vm(packed, F32),
            vm(per_head, BF16),
            vm(per_head, BF16),
            vm((n_groups, 8, 128), F32),
            vm(states, F32),
            vm(one_state, F32),
        ),
        in_specs=[anywhere] * 5,
        out_specs=(on_chip,) * 9,
        scratch_shapes=[
            vm((4,) + packed, BF16),
            vm((8, rows2, width), F32),
            vm(per_head, BF16),
            vm(per_head, BF16),
            vm(turned, BF16),
            vm(turned, BF16),
            vm(turned, BF16),
            vm(turned, BF16),
            vm((n_groups, GROUP, GROUP), F32),
            vm((n_heads, n_groups, GROUP, GROUP), BF16),
            vm((n_heads, GROUP, GROUP), BF16),
            vm(turned, F32),
            vm(turned, BF16),
            vm((2, rows2, width), F32),
            vm(states, F32),
            vm((n_heads, n_groups, width, width), BF16),
            vm(turned, BF16),
            vm(turned, BF16),
            pltpu.SMEM((2, n_groups), F32),
            pltpu.SMEM((2, n_seq), F32),
            pltpu.SMEM(doc_lengths.shape, jnp.int32),
            vm(slices, F32),
            vm(slices, F32),
            vm(one_state, F32),
            vm(slices, F32),
            vm(slices, F32),
            vm(sums, F32),
            vm((n_chunks, n_x * n_y, 2 * CHUNK, GROUP), F32),
            vm(sums, F32),
            vm(sums, F32),
            dma((4, n_groups // 2)),
        ]
        + [dma((n_heads,))] * 8
        + [dma((n_chunks,))] * 2
        + [dma],
        compiler_params=pltpu.CompilerParams(
            collective_id=0, has_side_effects=True, vmem_limit_bytes=44 << 20
        ),
        name="exchange_and_attend",
    )(doc_lengths, view(queries), view(keys), view(values), view(cotangent))
    mids = [pltpu.with_memory_space_constraint(m, pltpu.VMEM) for m in mids]
    results = pl.pallas_call(
        functools.partial(last_kernel, sizes),
        out_shape=(jax.ShapeDtypeStruct(packed, BF16),) * 4,
        in_specs=[on_chip] * 9,
        out_specs=(anywhere,) * 4,
        scratch_shapes=[
            vm((8, rows2, width), F32),
            vm((2,) + packed, BF16),
            dma((2, n_groups)),
            dma((2,)),
        ],
        compiler_params=pltpu.CompilerParams(vmem_limit_bytes=16 << 20),
        name="finish",
    )(*mids)
    return tuple(r.reshape(tokens_here, n_heads, width) for r in results)


def solution(mesh):
    n_x = 4
    spec = P("seq", "head", None)
    return jax.shard_map(
        functools.partial(per_device, (mesh.shape["seq"], n_x, mesh.shape["head"] // n_x)),
        mesh=mesh,
        in_specs=(spec,) * 4 + (P(),),
        out_specs=(spec,) * 4,
        check_vma=False,
    )
```
